32 devices in a mesh: px: 4 (over x, core), py: 8 (over z, y).
Axes of the slice: x: 2, y: 2, z: 4, core: 2. Of those that a mesh axis runs over, the one named last changes fastest.
Arguments:
- fraction: float32 [32, 64, 640], P('px', 'py'), may hold values from 0 to 1
- courant_x: float32 [32, 64, 640], P('px', 'py'), may hold values from -0.5 to 0.5
- courant_y: float32 [32, 64, 640], P('px', 'py'), may hold values from -0.5 to 0.5
- courant_z: float32 [32, 64, 640], P('px', 'py'), may hold values from -0.5 to 0.5
- labels: int32 [32, 64, 640], P('px', 'py'), may hold values from -1 to 31, as said below
- structure_owner: int32 [4, 32], P('px'), may hold values from 0 to 7, as said below
- parcel_owner: int32 [4, 32], P('px'), may hold values from 0 to 7, as said below
Outputs:
- remaining: float32 [32, 64, 640], P('px', 'py')
- moments: float32 [4, 13, 32], P('px', None, 'py')
- parcels: float32 [4, 13, 32], P('px', None, 'py')
The draws below stay inside these ranges and needn't reach their ends.
Inputs may be any that keep to these rules, and one draw needn't show every extreme that they name: `labels`: a label names a structure of the cell's row. `structure_owner`: in each row every index of py owns exactly 4 structures. `parcel_owner`: in each row every index of py receives exactly 4 parcels.
All inputs are finite; a program needn't handle non-finite values.
Results may differ from the reference program's by a relative error of at most 0.0003.
Values sent between devices are 32-bit elements; how exact they have to be, the bound alone decides.
A program may use at most 64 MiB of HBM per device.

```python
import jax
import jax.numpy as jnp
from jax import lax

CX = 8
CY = 8
NZ = 640
S_DEV = 4
NSY = 32
NX = 32
NY = 64
N_PX = 4
N_PY = 8


def box_table(key):
    shape = (N_PX, NSY)

    def side(tag, longest):
        octaves = max(2, longest.bit_length() - 1)
        octave = jax.random.randint(jax.random.fold_in(key, tag), shape, 1, octaves)
        lowest = jnp.left_shift(jnp.ones(shape, jnp.int32), octave)
        excess = jax.random.randint(jax.random.fold_in(key, tag + 1), shape, 0, lowest)
        return jnp.minimum(lowest + excess, longest).astype(jnp.int32)

    def corner(tag, length, extent):
        return jax.random.randint(jax.random.fold_in(key, tag), shape, 0, length - extent + 1).astype(jnp.int32)
    depth_reach = min(NZ, 128)
    dense = jax.random.randint(jax.random.fold_in(key, 13), shape, 0, 2).astype(jnp.int32)
    home = jax.random.randint(jax.random.fold_in(key, 14), (N_PX, 1), 0, N_PY).astype(jnp.int32)
    side_x = side(1, CX)
    thin_y = jax.random.randint(jax.random.fold_in(key, 15), shape, 1, 3).astype(jnp.int32)
    side_y = jnp.where(dense == 1, thin_y, side(3, 2 * CY)).astype(jnp.int32)
    side_z = jnp.where(dense == 1, side(17, min(NZ, 16)), side(5, depth_reach)).astype(jnp.int32)
    corner_x = corner(7, CX, side_x)
    spread_y = corner(8, NY, side_y)
    local_y = home * CY + jax.random.randint(jax.random.fold_in(key, 19), shape, 0, CY - side_y + 1)
    corner_y = jnp.where(dense == 1, local_y, spread_y).astype(jnp.int32)
    corner_z = corner(9, NZ, side_z)
    return (corner_x, side_x, corner_y, side_y, corner_z, side_z, dense)


def draw_labels(key, part):
    corner_x, side_x, corner_y, side_y, corner_z, side_z, dense = box_table(jax.random.fold_in(key, 31))
    reach_y = 2 * CY
    reach_z = min(NZ, 128)
    index_x = jnp.arange(CX, dtype=jnp.int32)[:, None, None]
    index_y = jnp.arange(reach_y, dtype=jnp.int32)[None, :, None]
    index_z = jnp.arange(reach_z, dtype=jnp.int32)[None, None, :]

    def one_row(row):

        def painter(phase):

            def place(which, canvas):
                start_y = jnp.minimum(corner_y[row, which], NY - reach_y).astype(jnp.int32)
                start_z = jnp.minimum(corner_z[row, which], NZ - reach_z).astype(jnp.int32)
                offset_y = corner_y[row, which] - start_y
                offset_z = corner_z[row, which] - start_z
                anchor = (jnp.int32(0), start_y, start_z)
                window = lax.dynamic_slice(canvas, anchor, (CX, reach_y, reach_z))
                inside = (index_x >= corner_x[row, which]) & (index_x < corner_x[row, which] + side_x[row, which])
                inside = inside & (index_y >= offset_y) & (index_y < offset_y + side_y[row, which])
                inside = inside & (index_z >= offset_z) & (index_z < offset_z + side_z[row, which])
                inside = inside & (dense[row, which] == phase)
                marked = jnp.where(inside, which, window).astype(jnp.int32)
                return lax.dynamic_update_slice(canvas, marked, anchor)
            return place
        canvas = jnp.full((CX, NY, NZ), -1, jnp.int32)
        canvas = lax.fori_loop(0, NSY, painter(0), canvas)
        return lax.fori_loop(0, NSY, painter(1), canvas)
    rows = lax.map(one_row, jnp.arange(N_PX, dtype=jnp.int32))
    return rows.reshape(NX, NY, NZ).astype(jnp.int32)


def owner_table(key):
    keys = jax.random.split(key, N_PX)

    def one_row(row_key):
        return jax.random.permutation(row_key, S_DEV * N_PY)
    return (jax.vmap(one_row)(keys) // S_DEV).astype(jnp.int32)


def draw_structure_owner(key, part):
    return owner_table(jax.random.fold_in(key, 11))


def draw_parcel_owner(key, part):
    return owner_table(jax.random.fold_in(key, 23))


def shard_levels(key, shape, shards, least, largest):
    def one(axis_at, parts):
        draws = jax.random.uniform(jax.random.fold_in(jax.random.fold_in(key, 6), axis_at), (parts,), jnp.float32, least / len(shards), largest / len(shards))
        return jnp.repeat(jnp.exp(draws), shape[axis_at] // parts).reshape((-1,) + (1,) * (len(shape) - axis_at - 1))

    level = one(*shards[0])
    for cut in shards[1:]:
        level = level * one(*cut)
    return level


def setup_inputs(seed: int = 0) -> dict:
    seeds = jax.random.split(jax.random.key(seed), 8)
    return {
        "fraction": jnp.clip(1.0 * jax.random.uniform(seeds[0], (NX, NY, NZ), jnp.float32) ** shard_levels(seeds[0], (NX, NY, NZ), ((0, 4), (1, 8)), -0.2, 0.2), 0.0, 1.0),
        "courant_x": jnp.clip(jax.random.uniform(seeds[1], (NX, NY, NZ), jnp.float32, -0.5, 0.5) * shard_levels(seeds[1], (NX, NY, NZ), ((0, 4), (1, 8)), -0.4, 0.0), -0.5, 0.5),
        "courant_y": jnp.clip(jax.random.uniform(seeds[2], (NX, NY, NZ), jnp.float32, -0.5, 0.5) * shard_levels(seeds[2], (NX, NY, NZ), ((0, 4), (1, 8)), -0.4, 0.0), -0.5, 0.5),
        "courant_z": jnp.clip(jax.random.uniform(seeds[3], (NX, NY, NZ), jnp.float32, -0.5, 0.5) * shard_levels(seeds[3], (NX, NY, NZ), ((0, 4), (1, 8)), -0.4, 0.0), -0.5, 0.5),
        "labels": draw_labels(jax.random.fold_in(seeds[7], 71), 0),
        "structure_owner": draw_structure_owner(jax.random.fold_in(seeds[7], 71), 0),
        "parcel_owner": draw_parcel_owner(jax.random.fold_in(seeds[7], 71), 0),
    }


def advance(padded_frac, padded_cour, length, axis):
    def part(array, start, count):
        return lax.slice_in_dim(array, start, start + count, axis=axis)
    centre = part(padded_frac, 1, length + 2)
    spread = 0.5 * (part(padded_frac, 2, length + 2) - part(padded_frac, 0, length + 2))
    bound = 2.0 * jnp.minimum(centre, 1.0 - centre)
    slope = jnp.minimum(jnp.maximum(spread, -bound), bound)
    courant = part(padded_cour, 1, length + 1)
    upwind = part(centre, 0, length + 1) + 0.5 * (1.0 - courant) * part(slope, 0, length + 1)
    downwind = part(centre, 1, length + 1) - 0.5 * (1.0 + courant) * part(slope, 1, length + 1)
    flux = courant * jnp.where(courant > 0.0, upwind, downwind)
    middle = part(padded_frac, 2, length)
    high = part(courant, 1, length)
    low = part(courant, 0, length)
    updated = middle - (part(flux, 1, length) - part(flux, 0, length)) + middle * (high - low)
    return updated, 0.5 * (high + low)


def parcel_rows(moment_rows):
    volume = moment_rows[0]
    safe = jnp.maximum(volume, 0.5)
    centre = moment_rows[1:4] / safe
    velocity = moment_rows[4:7] / safe
    square = moment_rows[7:10] / safe - centre * centre
    cross = jnp.stack([moment_rows[10] / safe - centre[0] * centre[1],
                       moment_rows[11] / safe - centre[0] * centre[2],
                       moment_rows[12] / safe - centre[1] * centre[2]])
    return jnp.concatenate([volume[None], centre, velocity, square, cross], 0)


def slot_of(owner_row):
    count = owner_row.shape[0]
    index = jnp.arange(count, dtype=jnp.int32)
    same = owner_row[:, None] == owner_row[None, :]
    earlier = index[None, :] < index[:, None]
    rank = jnp.sum((same & earlier).astype(jnp.int32), axis=1)
    return (owner_row * S_DEV + rank).astype(jnp.int32)


def reference(fraction, courant_x, courant_y, courant_z, labels, structure_owner, parcel_owner):
    wrap_x = ((2, 2), (0, 0), (0, 0))
    first, velocity_x = advance(jnp.pad(fraction, wrap_x, mode="wrap"), jnp.pad(courant_x, wrap_x, mode="wrap"), NX, 0)
    pad_y = ((0, 0), (2, 2), (0, 0))
    second, velocity_y = advance(jnp.pad(first, pad_y), jnp.pad(courant_y, pad_y), NY, 1)
    pad_z = ((0, 0), (0, 0), (2, 2))
    third, velocity_z = advance(jnp.pad(second, pad_z), jnp.pad(courant_z, pad_z), NZ, 2)
    remaining = jnp.where(labels >= 0, jnp.float32(0.0), third)
    scale = 4.0 / (CX * CY * CY)

    def row_moments(row):
        start = (row * CX).astype(jnp.int32)
        def take(array):
            return lax.dynamic_slice_in_dim(array, start, CX, 0)
        weight = take(third) * scale
        coord_x = ((start + jnp.arange(CX, dtype=jnp.int32)).astype(jnp.float32) + 0.5)[:, None, None] / NX
        coord_y = (jnp.arange(NY, dtype=jnp.int32).astype(jnp.float32) + 0.5)[None, :, None] / NY
        coord_z = (jnp.arange(NZ, dtype=jnp.int32).astype(jnp.float32) + 0.5)[None, None, :] / NZ
        shape = weight.shape
        pieces = [jnp.ones(shape, jnp.float32), coord_x, coord_y, coord_z,
                  take(velocity_x), take(velocity_y), take(velocity_z),
                  coord_x * coord_x, coord_y * coord_y, coord_z * coord_z,
                  coord_x * coord_y, coord_x * coord_z, coord_y * coord_z]
        features = jnp.stack([(weight * jnp.broadcast_to(piece, shape)).reshape(-1) for piece in pieces], 1)
        marks = take(labels).reshape(-1)
        ids = jnp.where(marks >= 0, marks, NSY).astype(jnp.int32)
        summed = jax.ops.segment_sum(features, ids, num_segments=NSY + 1)
        return summed[:NSY].T

    raw = lax.map(row_moments, jnp.arange(N_PX, dtype=jnp.int32))

    def place(values, owner_row):
        return jnp.zeros((13, NSY), jnp.float32).at[:, slot_of(owner_row)].set(values)

    moments = jax.vmap(place)(raw, structure_owner)
    parcels = jax.vmap(place)(jax.vmap(parcel_rows)(raw), parcel_owner)
    return remaining, moments, parcels
```

```python
import functools

import jax
import jax.numpy as jnp
from jax import lax
from jax.experimental import pallas as pl
from jax.experimental.pallas import tpu as pltpu
from jax.sharding import PartitionSpec as P

MESH = pl.DeviceIdType.MESH
FEATURES = 9


def slope_of(before, centre, after):
    bound = 2.0 * jnp.minimum(centre, 1.0 - centre)
    return jnp.minimum(jnp.maximum(0.5 * (after - before), -bound), bound)


def flux_of(courant, f_low, s_low, f_high, s_high):
    positive = courant > 0.0
    donor = jnp.where(positive, f_low, f_high)
    slope = jnp.where(positive, s_low, -s_high)
    return courant * (donor + 0.5 * (1.0 - jnp.abs(courant)) * slope)


def slot_row(owner, per_owner):
    count = owner.shape[1]
    rows = lax.broadcasted_iota(jnp.int32, (count, count), 0)
    columns = lax.broadcasted_iota(jnp.int32, (count, count), 1)
    wide = jnp.broadcast_to(owner, (count, count)).astype(jnp.float32)
    column = jnp.sum(jnp.where(rows == columns, wide, 0.0), axis=1, keepdims=True)
    earlier = (wide == column) & (rows < columns)
    rank = jnp.sum(jnp.where(earlier, 1.0, 0.0), axis=0, keepdims=True)
    return owner.astype(jnp.float32) * per_owner + rank


def kernel(
    n_px, n_py,
    f_in, cx_in, cy_in, cz_in, lab_in, so_ref, po_ref,
    rem_out, mom_ref, par_ref,
    p_ref, h_ref, c_ref, ch_ref, cy_ref, cyh_ref, cz_ref, lab_ref, hot_ref, acc_ref,
    rem_ref, row_ref, part_ref, slots_ref,
    local_sem, halo_send, halo_recv, part_send, part_recv,
):
    size_x, size_y, depth = f_in.shape
    structures = so_ref.shape[1]
    per_owner = structures // n_py
    px = lax.axis_index("px")
    py = lax.axis_index("py")
    has_low = py > 0
    has_high = py < n_py - 1

    loads = [
        (lab_in, lab_ref),
        (f_in, p_ref.at[pl.ds(2, size_x)]),
        (cx_in, c_ref.at[pl.ds(1, size_x)]),
        (cy_in, cy_ref),
        (cz_in, cz_ref),
    ]
    copies = [pltpu.make_async_copy(s, d, local_sem.at[k]) for k, (s, d) in enumerate(loads)]
    for copy in copies:
        copy.start()

    def device(dx, dy):
        return (lax.rem(px + dx + n_px, n_px), py + dy)

    barrier = pltpu.get_barrier_semaphore()

    def greet(where):
        pl.semaphore_signal(barrier, inc=1, device_id=where, device_id_type=MESH)

    def peer(step):
        return lax.rem(py + step, n_py)

    for step in range(1, n_py):
        greet((px, peer(step)))
    for dx in (-1, 1):
        greet(device(dx, 0))

    @pl.when(has_low)
    def _():
        greet(device(-1, -1))
        greet(device(1, -1))

    @pl.when(has_high)
    def _():
        greet(device(-1, 1))
        greet(device(1, 1))

    callers = n_py + 1 + jnp.where(has_low, 2, 0) + jnp.where(has_high, 2, 0)
    pl.semaphore_wait(barrier, callers)

    end_x, end_y = size_x - 2, size_y - 2
    last_x, low, high = pl.ds(size_x - 1, 1), pl.ds(end_y, 2), pl.ds(0, 2)
    all_x, all_c = pl.ds(2, size_x), pl.ds(1, size_x)
    top_f, bottom_f = pl.ds(end_x, 2), pl.ds(0, 2)
    beyond = pl.ds(size_x + 2, 2)
    moves = []
    for dy, rows in ((1, low), (-1, high)):
        moves.append((f_in.at[top_f, rows], h_ref.at[pl.ds(0, 2), rows], 1, dy))
        moves.append((f_in.at[bottom_f, rows], h_ref.at[beyond, rows], -1, dy))
        moves.append((cx_in.at[last_x, rows], ch_ref.at[pl.ds(0, 1), rows], 1, dy))
    for dy, rows in ((1, low), (-1, high)):
        moves.append((f_in.at[:, rows], h_ref.at[all_x, rows], 0, dy))
        moves.append((cx_in.at[:, rows], ch_ref.at[all_c, rows], 0, dy))
    last_y = pl.ds(size_y - 1, 1)
    moves.append((cy_in.at[:, last_y], cyh_ref.at[:, last_y], 0, 1))
    moves.append((f_in.at[top_f], p_ref.at[pl.ds(0, 2)], 1, 0))
    moves.append((cx_in.at[last_x], c_ref.at[pl.ds(0, 1)], 1, 0))
    moves.append((f_in.at[bottom_f], p_ref.at[beyond], -1, 0))

    remote = [
        pltpu.make_async_remote_copy(
            src_ref=source, dst_ref=target, send_sem=halo_send.at[k], recv_sem=halo_recv.at[k],
            device_id=device(dx, dy), device_id_type=MESH,
        )
        for k, (source, target, dx, dy) in enumerate(moves)
    ]

    def for_rows(dy, action):
        chosen = [copy for copy, move in zip(remote, moves) if move[3] == dy]

        def run():
            for copy in chosen:
                action(copy)

        if dy == 0:
            run()
        else:
            sends = action is start_copy or action is wait_sent
            pl.when(has_high if (dy > 0) == sends else has_low)(run)

    def start_copy(copy):
        copy.start()

    def wait_sent(copy):
        copy.wait_send()

    def wait_arrived(copy):
        copy.wait_recv()

    for dy in (1, -1, 0):
        for_rows(dy, start_copy)

    copies[0].wait()
    names = lax.broadcasted_iota(jnp.int32, (structures, depth), 0)

    def mark(i, carry):
        for j in range(size_y):
            line = jnp.broadcast_to(lab_ref[i, pl.ds(j, 1), :], (structures, depth))
            hot = jnp.where(line == names, 1.0, 0.0).astype(jnp.bfloat16)
            hot_ref[i, pl.ds(j * structures, structures), :] = hot
        return carry

    lax.fori_loop(0, size_x, mark, 0)
    owned_slots = slot_row(so_ref[...], per_owner)
    parcel_slots = slot_row(po_ref[...], per_owner)

    for copy in copies[1:]:
        copy.wait()
    for dy in (1, -1, 0):
        for_rows(dy, wait_arrived)

    plane = (size_y, depth)
    sub = lax.broadcasted_iota(jnp.int32, plane, 0)
    lane = lax.broadcasted_iota(jnp.int32, plane, 1)
    first_row, last_row = sub == 0, sub == size_y - 1
    first_cell, last_cell = lane == 0, lane == depth - 1
    low_limit = jnp.where(has_low, end_y, size_y)
    high_limit = jnp.where(has_high, 2, 0)
    halo_valid = (sub >= low_limit) | (sub < high_limit)
    coord_z = (lane.astype(jnp.float32) + 0.5) / depth
    scale = 4.0 / (size_x * size_y * size_y)

    def next_y(main, other):
        return pltpu.roll(jnp.where(first_row, other, main), size_y - 1, 0)

    def prior_y(main, other):
        return pltpu.roll(jnp.where(last_row, other, main), 1, 0)

    def next_z(value):
        return jnp.where(last_cell, 0.0, pltpu.roll(value, depth - 1, 1))

    def prior_z(value):
        return jnp.where(first_cell, 0.0, pltpu.roll(value, 1, 1))

    class Along:
        def __init__(self, frac, cour):
            self.frac, self.cour = frac, cour
            before = slope_of(frac[0], frac[1], frac[2])
            self.slope = slope_of(frac[1], frac[2], frac[3])
            self.flux = flux_of(cour[0], frac[1], before, frac[2], self.slope)

        def layer(self, i):
            frac, here, below = self.frac[i + 2], self.cour[i + 1], self.cour[i]
            later = self.frac[i + 3]
            slope = slope_of(frac, later, self.frac[i + 4])
            flux = flux_of(here, frac, self.slope, later, slope)
            result = frac - (flux - self.flux) + frac * (here - below)
            self.slope, self.flux = slope, flux
            return result, 0.5 * (here + below)

    main_x, halo_x = Along(p_ref, c_ref), Along(h_ref, ch_ref)
    for i in range(size_x):
        first, velocity_x = main_x.layer(i)
        outer, _ = halo_x.layer(i)
        outer = jnp.where(halo_valid, outer, 0.0)

        c = cy_ref[i]
        c_outer = jnp.where(halo_valid, cyh_ref[i], 0.0)
        after, after_outer = next_y(first, outer), next_y(outer, first)
        slope = slope_of(prior_y(first, outer), first, after)
        slope_outer = slope_of(prior_y(outer, first), outer, after_outer)
        flux = flux_of(c, first, slope, after, next_y(slope, slope_outer))
        flux_outer = flux_of(c_outer, outer, slope_outer, after_outer, next_y(slope_outer, slope))
        below = prior_y(c, c_outer)
        second = first - (flux - prior_y(flux, flux_outer)) + first * (c - below)
        velocity_y = 0.5 * (c + below)

        c = cz_ref[i]
        after = next_z(second)
        slope = slope_of(prior_z(second), second, after)
        flux = flux_of(c, second, slope, after, next_z(slope))
        below = prior_z(c)
        third = second - (flux - prior_z(flux)) + second * (c - below)
        velocity_z = 0.5 * (c + below)

        rem_ref[i] = jnp.where(lab_ref[i] >= 0, 0.0, third)
        coord_x = ((px * size_x + i).astype(jnp.float32) + 0.5) / (size_x * n_px)
        w = third * scale
        wx, wz = w * coord_x, w * coord_z
        features = [w, wx, wx * coord_x, wz, wx * coord_z, wz * coord_z,
                    w * velocity_x, w * velocity_y, w * velocity_z]
        parts = []
        for value in features:
            parts.append(value)
            parts.append(value - value.astype(jnp.bfloat16).astype(jnp.float32))
        left = jnp.concatenate(parts, axis=0).astype(jnp.bfloat16)
        sums = lax.dot_general(left, hot_ref[i], (((1,), (1,)), ((), ())),
                               preferred_element_type=jnp.float32)
        if i == 0:
            acc_ref[...] = sums
        else:
            acc_ref[...] += sums

    store = pltpu.make_async_copy(rem_ref, rem_out, local_sem.at[len(loads)])
    store.start()

    width = size_y * structures
    sub = lax.broadcasted_iota(jnp.int32, (size_y, width), 0)
    lane = lax.broadcasted_iota(jnp.int32, (size_y, width), 1)
    mine = (lane >= sub * structures) & (lane < (sub + 1) * structures)
    coord_y = ((py * size_y + sub).astype(jnp.float32) + 0.5) / (size_y * n_py)

    def collect(k):
        base = 2 * size_y * k
        both = acc_ref[pl.ds(base, size_y), :] + acc_ref[pl.ds(base + size_y, size_y), :]
        return jnp.where(mine, both, 0.0)

    def put(row, value):
        row_ref[pl.ds(row, 1), :] = jnp.sum(value, axis=0, keepdims=True)

    row_ref[...] = jnp.zeros_like(row_ref)
    w, wx, wxx, wz, wxz, wzz, ux, uy, uz = [collect(k) for k in range(FEATURES)]
    wy = w * coord_y
    for row, value in enumerate((w, wx, wy, wz, ux, uy, uz, wxx, wy * coord_y, wzz,
                                 wx * coord_y, wxz, wz * coord_y)):
        put(row, value)
    total = row_ref[:, pl.ds(0, structures)]
    for j in range(1, size_y):
        total = total + row_ref[:, pl.ds(j * structures, structures)]
    part_ref[...] = total
    slots_ref[py] = total

    sends = []
    for step in range(1, n_py):
        copy = pltpu.make_async_remote_copy(
            src_ref=part_ref, dst_ref=slots_ref.at[py],
            send_sem=part_send.at[step], recv_sem=part_recv.at[py],
            device_id=(px, peer(step)), device_id_type=MESH,
        )
        copy.start()
        sends.append(copy)
    for dy in (1, -1, 0):
        for_rows(dy, wait_sent)
    for step in range(1, n_py):
        source = peer(step)
        pltpu.make_async_remote_copy(
            src_ref=part_ref, dst_ref=slots_ref.at[source],
            send_sem=part_send.at[step], recv_sem=part_recv.at[source],
            device_id=(px, source), device_id_type=MESH,
        ).wait_recv()

    total = slots_ref[0]
    for k in range(1, n_py):
        total = total + slots_ref[k]

    def pick(slots):
        where = lax.broadcasted_iota(jnp.int32, (total.shape[0], per_owner), 1)
        result = jnp.zeros((total.shape[0], per_owner), jnp.float32)
        for j in range(per_owner):
            chosen = slots == (py * per_owner + j).astype(jnp.float32)
            column = jnp.sum(jnp.where(chosen, total, 0.0), axis=1, keepdims=True)
            result = jnp.where(where == j, column, result)
        return result

    mom_ref[0] = pick(owned_slots)[:13]
    m = pick(parcel_slots)
    volume = m[0:1]
    safe = jnp.maximum(volume, 0.5)
    centre = m[1:4] / safe
    velocity = m[4:7] / safe
    square = m[7:10] / safe - centre * centre
    par_ref[0, 0:1] = volume
    par_ref[0, 1:4] = centre
    par_ref[0, 4:7] = velocity
    par_ref[0, 7:10] = square
    par_ref[0, 10:11] = m[10:11] / safe - centre[0:1] * centre[1:2]
    par_ref[0, 11:12] = m[11:12] / safe - centre[0:1] * centre[2:3]
    par_ref[0, 12:13] = m[12:13] / safe - centre[1:2] * centre[2:3]

    store.wait()
    for copy in sends:
        copy.wait_send()


def local(n_px, n_py, fraction, courant_x, courant_y, courant_z, labels, structure_owner, parcel_owner):
    size_x, size_y, depth = fraction.shape
    structures = structure_owner.shape[1]
    per_owner = structures // n_py
    f32 = jnp.float32
    block = (size_x, size_y, depth)
    rows = 16
    moves = 14
    any_spec = pl.BlockSpec(memory_space=pl.ANY)
    vmem = pl.BlockSpec(memory_space=pltpu.VMEM)
    dma = pltpu.SemaphoreType.DMA
    return pl.pallas_call(
        functools.partial(kernel, n_px, n_py),
        out_shape=(
            jax.ShapeDtypeStruct(block, f32),
            jax.ShapeDtypeStruct((1, 13, per_owner), f32),
            jax.ShapeDtypeStruct((1, 13, per_owner), f32),
        ),
        in_specs=[any_spec] * 5 + [vmem] * 2,
        out_specs=(any_spec, vmem, vmem),
        scratch_shapes=[
            pltpu.VMEM((size_x + 4, size_y, depth), f32),
            pltpu.VMEM((size_x + 4, size_y, depth), f32),
            pltpu.VMEM((size_x + 1, size_y, depth), f32),
            pltpu.VMEM((size_x + 1, size_y, depth), f32),
            pltpu.VMEM(block, f32),
            pltpu.VMEM(block, f32),
            pltpu.VMEM(block, f32),
            pltpu.VMEM(block, jnp.int32),
            pltpu.VMEM((size_x, size_y * structures, depth), jnp.bfloat16),
            pltpu.VMEM((FEATURES * 2 * size_y, size_y * structures), f32),
            pltpu.VMEM(block, f32),
            pltpu.VMEM((rows, size_y * structures), f32),
            pltpu.VMEM((rows, structures), f32),
            pltpu.VMEM((n_py, rows, structures), f32),
            dma((6,)),
            dma((moves,)),
            dma((moves,)),
            dma((n_py,)),
            dma((n_py,)),
        ],
        compiler_params=pltpu.CompilerParams(collective_id=0, has_side_effects=True),
    )(fraction, courant_x, courant_y, courant_z, labels, structure_owner, parcel_owner)


def solution(mesh):
    return jax.shard_map(
        functools.partial(local, mesh.shape["px"], mesh.shape["py"]),
        mesh=mesh,
        in_specs=(P("px", "py", None),) * 5 + (P("px", None),) * 2,
        out_specs=(P("px", "py", None), P("px", None, "py"), P("px", None, "py")),
        check_vma=False,
    )
```

```python
import functools

import jax
import jax.numpy as jnp
from jax import lax
from jax.experimental import pallas as pl
from jax.experimental.pallas import tpu as pltpu
from jax.sharding import PartitionSpec as P

MESH = pl.DeviceIdType.MESH
FEATURES = 9
ROWS = 16


def slope_of(before, centre, after):
    bound = 2.0 * jnp.minimum(centre, 1.0 - centre)
    return jnp.minimum(jnp.maximum(0.5 * (after - before), -bound), bound)


def flux_of(courant, f_low, s_low, f_high, s_high):
    positive = courant > 0.0
    donor = jnp.where(positive, f_low, f_high)
    slope = jnp.where(positive, s_low, -s_high)
    return courant * (donor + 0.5 * (1.0 - jnp.abs(courant)) * slope)


def slot_row(owner, per_owner):
    count = owner.shape[1]
    rows = lax.broadcasted_iota(jnp.int32, (count, count), 0)
    columns = lax.broadcasted_iota(jnp.int32, (count, count), 1)
    wide = jnp.broadcast_to(owner, (count, count)).astype(jnp.float32)
    column = jnp.sum(jnp.where(rows == columns, wide, 0.0), axis=1, keepdims=True)
    earlier = (wide == column) & (rows < columns)
    rank = jnp.sum(jnp.where(earlier, 1.0, 0.0), axis=0, keepdims=True)
    return owner.astype(jnp.float32) * per_owner + rank


def pack_groups(structures):
    return 128 // structures if structures < 128 and 128 % structures == 0 and structures >= 8 else 1


def packed(row_ref, structures):
    width = row_ref.shape[1]
    groups = pack_groups(structures)
    if groups == 1 or width % 128:
        total = row_ref[:, pl.ds(0, structures)]
        for j in range(1, width // structures):
            total = total + row_ref[:, pl.ds(j * structures, structures)]
        if groups == 1:
            return total
        total = jnp.concatenate([total] * groups, axis=1)
    else:
        total = row_ref[:, pl.ds(0, 128)]
        for j in range(1, width // 128):
            total = total + row_ref[:, pl.ds(j * 128, 128)]
        shift = 64
        while shift >= structures:
            total = total + pltpu.roll(total, shift, 1)
            shift //= 2
    rows = ROWS // groups
    lane = lax.broadcasted_iota(jnp.int32, (rows, 128), 1)
    result = total[:rows]
    for k in range(1, groups):
        result = jnp.where(lane >= k * structures, total[k * rows : (k + 1) * rows], result)
    return result


def kernel(
    n_px, n_py,
    structures,
    f_in, cx_in, cy_in, cz_in, lab_in, so_in, po_in,
    rem_ref, total_ref, place_ref,
    p_ref, h_ref, c_ref, ch_ref, cy_ref, cyh_ref, cz_ref, lab_ref, hot_ref, acc_ref,
    row_ref, part_ref, slots_ref, so_ref, po_ref,
    local_sem, halo_send, halo_recv, part_send, part_recv,
):
    size_x, size_y, depth = f_in.shape
    px = lax.axis_index("px")
    py = lax.axis_index("py")
    has_low = py > 0
    has_high = py < n_py - 1

    def device(dx, dy):
        return (lax.rem(px + dx + n_px, n_px), py + dy)

    barrier = pltpu.get_barrier_semaphore()

    def greet(where):
        pl.semaphore_signal(barrier, inc=1, device_id=where, device_id_type=MESH)

    def peer(step):
        return lax.rem(py + step, n_py)

    for step in range(1, n_py):
        greet((px, peer(step)))
    for dx in (-1, 1):
        greet(device(dx, 0))

    @pl.when(has_low)
    def _():
        greet(device(-1, -1))
        greet(device(1, -1))

    @pl.when(has_high)
    def _():
        greet(device(-1, 1))
        greet(device(1, 1))

    loads = [
        (lab_in, lab_ref),
        (f_in, p_ref.at[pl.ds(2, size_x)]),
        (cx_in, c_ref.at[pl.ds(1, size_x)]),
        (cy_in, cy_ref),
        (cz_in, cz_ref),
        (so_in, so_ref),
        (po_in, po_ref),
    ]
    copies = [pltpu.make_async_copy(s, d, local_sem.at[k]) for k, (s, d) in enumerate(loads)]
    for copy in copies:
        copy.start()

    callers = n_py + 1 + jnp.where(has_low, 2, 0) + jnp.where(has_high, 2, 0)
    pl.semaphore_wait(barrier, callers)

    end_x, end_y = size_x - 2, size_y - 2
    last_x, low, high = pl.ds(size_x - 1, 1), pl.ds(end_y, 2), pl.ds(0, 2)
    all_x, all_c = pl.ds(2, size_x), pl.ds(1, size_x)
    top_f, bottom_f = pl.ds(end_x, 2), pl.ds(0, 2)
    beyond = pl.ds(size_x + 2, 2)
    moves = []
    for dy, rows in ((1, low), (-1, high)):
        moves.append((f_in.at[top_f, rows], h_ref.at[pl.ds(0, 2), rows], 1, dy))
        moves.append((f_in.at[bottom_f, rows], h_ref.at[beyond, rows], -1, dy))
        moves.append((cx_in.at[last_x, rows], ch_ref.at[pl.ds(0, 1), rows], 1, dy))
    for dy, rows in ((1, low), (-1, high)):
        moves.append((f_in.at[:, rows], h_ref.at[all_x, rows], 0, dy))
        moves.append((cx_in.at[:, rows], ch_ref.at[all_c, rows], 0, dy))
    last_y = pl.ds(size_y - 1, 1)
    moves.append((cy_in.at[:, last_y], cyh_ref.at[:, last_y], 0, 1))
    moves.append((f_in.at[top_f], p_ref.at[pl.ds(0, 2)], 1, 0))
    moves.append((cx_in.at[last_x], c_ref.at[pl.ds(0, 1)], 1, 0))
    moves.append((f_in.at[bottom_f], p_ref.at[beyond], -1, 0))

    remote = [
        pltpu.make_async_remote_copy(
            src_ref=source, dst_ref=target, send_sem=halo_send.at[k], recv_sem=halo_recv.at[k],
            device_id=device(dx, dy), device_id_type=MESH,
        )
        for k, (source, target, dx, dy) in enumerate(moves)
    ]

    def for_rows(dy, action):
        chosen = [copy for copy, move in zip(remote, moves) if move[3] == dy]

        def run():
            for copy in chosen:
                action(copy)

        if dy == 0:
            run()
        else:
            sends = action is start_copy or action is wait_sent
            pl.when(has_high if (dy > 0) == sends else has_low)(run)

    def start_copy(copy):
        copy.start()

    def wait_sent(copy):
        copy.wait_send()

    def wait_arrived(copy):
        copy.wait_recv()

    for dy in (1, -1, 0):
        for_rows(dy, start_copy)

    copies[0].wait()
    names = lax.broadcasted_iota(jnp.int32, (structures, depth), 0)

    def mark(i, carry):
        for j in range(size_y):
            line = jnp.broadcast_to(lab_ref[i, pl.ds(j, 1), :], (structures, depth))
            hot = jnp.where(line == names, 1.0, 0.0).astype(jnp.bfloat16)
            hot_ref[i, pl.ds(j * structures, structures), :] = hot
        return carry

    lax.fori_loop(0, size_x, mark, 0)

    for copy in copies[1:]:
        copy.wait()
    place_ref[0:1] = slot_row(so_ref[...], structures // n_py)
    place_ref[1:2] = slot_row(po_ref[...], structures // n_py)
    for dy in (1, -1, 0):
        for_rows(dy, wait_arrived)

    plane = (size_y, depth)
    sub = lax.broadcasted_iota(jnp.int32, plane, 0)
    lane = lax.broadcasted_iota(jnp.int32, plane, 1)
    first_row, last_row = sub == 0, sub == size_y - 1
    first_cell, last_cell = lane == 0, lane == depth - 1
    low_limit = jnp.where(has_low, end_y, size_y)
    high_limit = jnp.where(has_high, 2, 0)
    halo_valid = (sub >= low_limit) | (sub < high_limit)
    coord_z = (lane.astype(jnp.float32) + 0.5) / depth
    scale = 4.0 / (size_x * size_y * size_y)

    def next_y(main, other):
        return pltpu.roll(jnp.where(first_row, other, main), size_y - 1, 0)

    def prior_y(main, other):
        return pltpu.roll(jnp.where(last_row, other, main), 1, 0)

    def next_z(value):
        return jnp.where(last_cell, 0.0, pltpu.roll(value, depth - 1, 1))

    def prior_z(value):
        return jnp.where(first_cell, 0.0, pltpu.roll(value, 1, 1))

    class Along:
        def __init__(self, frac, cour):
            self.frac, self.cour = frac, cour
            before = slope_of(frac[0], frac[1], frac[2])
            self.slope = slope_of(frac[1], frac[2], frac[3])
            self.flux = flux_of(cour[0], frac[1], before, frac[2], self.slope)

        def layer(self, i):
            frac, here, below = self.frac[i + 2], self.cour[i + 1], self.cour[i]
            later = self.frac[i + 3]
            slope = slope_of(frac, later, self.frac[i + 4])
            flux = flux_of(here, frac, self.slope, later, slope)
            result = frac - (flux - self.flux) + frac * (here - below)
            self.slope, self.flux = slope, flux
            return result, 0.5 * (here + below)

    main_x, halo_x = Along(p_ref, c_ref), Along(h_ref, ch_ref)
    for i in range(size_x):
        first, velocity_x = main_x.layer(i)
        outer, _ = halo_x.layer(i)
        outer = jnp.where(halo_valid, outer, 0.0)

        c = cy_ref[i]
        c_outer = jnp.where(halo_valid, cyh_ref[i], 0.0)
        after, after_outer = next_y(first, outer), next_y(outer, first)
        slope = slope_of(prior_y(first, outer), first, after)
        slope_outer = slope_of(prior_y(outer, first), outer, after_outer)
        flux = flux_of(c, first, slope, after, next_y(slope, slope_outer))
        flux_outer = flux_of(c_outer, outer, slope_outer, after_outer, next_y(slope_outer, slope))
        below = prior_y(c, c_outer)
        second = first - (flux - prior_y(flux, flux_outer)) + first * (c - below)
        velocity_y = 0.5 * (c + below)

        c = cz_ref[i]
        after = next_z(second)
        slope = slope_of(prior_z(second), second, after)
        flux = flux_of(c, second, slope, after, next_z(slope))
        below = prior_z(c)
        third = second - (flux - prior_z(flux)) + second * (c - below)
        velocity_z = 0.5 * (c + below)

        rem_ref[i] = jnp.where(lab_ref[i] >= 0, 0.0, third)
        coord_x = ((px * size_x + i).astype(jnp.float32) + 0.5) / (size_x * n_px)
        w = third * scale
        wx, wz = w * coord_x, w * coord_z
        features = [w, wx, wx * coord_x, wz, wx * coord_z, wz * coord_z,
                    w * velocity_x, w * velocity_y, w * velocity_z]
        parts = []
        for value in features:
            parts.append(value)
            parts.append(value - value.astype(jnp.bfloat16).astype(jnp.float32))
        left = jnp.concatenate(parts, axis=0).astype(jnp.bfloat16)
        sums = lax.dot_general(left, hot_ref[i], (((1,), (1,)), ((), ())),
                               preferred_element_type=jnp.float32)
        if i == 0:
            acc_ref[...] = sums
        else:
            acc_ref[...] += sums

    width = size_y * structures
    sub = lax.broadcasted_iota(jnp.int32, (size_y, width), 0)
    lane = lax.broadcasted_iota(jnp.int32, (size_y, width), 1)
    mine = (lane >= sub * structures) & (lane < (sub + 1) * structures)
    coord_y = ((py * size_y + sub).astype(jnp.float32) + 0.5) / (size_y * n_py)

    def collect(k):
        base = 2 * size_y * k
        both = acc_ref[pl.ds(base, size_y), :] + acc_ref[pl.ds(base + size_y, size_y), :]
        return jnp.where(mine, both, 0.0)

    def put(row, value):
        row_ref[pl.ds(row, 1), :] = jnp.sum(value, axis=0, keepdims=True)

    row_ref[...] = jnp.zeros_like(row_ref)
    w, wx, wxx, wz, wxz, wzz, ux, uy, uz = [collect(k) for k in range(FEATURES)]
    wy = w * coord_y
    for row, value in enumerate((w, wx, wy, wz, ux, uy, uz, wxx, wy * coord_y, wzz,
                                 wx * coord_y, wxz, wz * coord_y)):
        put(row, value)
    total = packed(row_ref, structures)
    part_ref[...] = total
    slots_ref[py] = total

    sends = []
    for step in range(1, n_py):
        copy = pltpu.make_async_remote_copy(
            src_ref=part_ref, dst_ref=slots_ref.at[py],
            send_sem=part_send.at[step], recv_sem=part_recv.at[py],
            device_id=(px, peer(step)), device_id_type=MESH,
        )
        copy.start()
        sends.append(copy)
    for dy in (1, -1, 0):
        for_rows(dy, wait_sent)
    for step in range(1, n_py):
        source = peer(step)
        pltpu.make_async_remote_copy(
            src_ref=part_ref, dst_ref=slots_ref.at[source],
            send_sem=part_send.at[step], recv_sem=part_recv.at[source],
            device_id=(px, source), device_id_type=MESH,
        ).wait_recv()

    total = slots_ref[0]
    for k in range(1, n_py):
        total = total + slots_ref[k]

    total_ref[...] = total
    for copy in sends:
        copy.wait_send()


def finish(n_py, rem_in, total_ref, place_ref, rem_out, mom_ref, par_ref, sem):
    store = pltpu.make_async_copy(rem_in, rem_out, sem)
    store.start()
    structures = place_ref.shape[1]
    per_owner = structures // n_py
    py = lax.axis_index("py")
    groups = pack_groups(structures)
    total = total_ref[...]
    if groups > 1:
        total = jnp.concatenate([total[:, k * structures : (k + 1) * structures] for k in range(groups)], axis=0)

    def pick(slots):
        wanted = lax.broadcasted_iota(jnp.int32, (per_owner, structures), 0) + py * per_owner
        chosen = jnp.where(slots == wanted.astype(jnp.float32), 1.0, 0.0)
        return lax.dot_general(chosen, total, (((1,), (1,)), ((), ())),
                               precision=lax.Precision.HIGHEST, preferred_element_type=jnp.float32)

    mom_ref[0] = pick(place_ref[0:1])[:, :13]
    m = pick(place_ref[1:2])
    volume = m[:, 0:1]
    q = m / jnp.maximum(volume, 0.5)
    centre = q[:, 1:4]
    par_ref[0, :, 0:1] = volume
    par_ref[0, :, 1:7] = q[:, 1:7]
    par_ref[0, :, 7:10] = q[:, 7:10] - centre * centre
    par_ref[0, :, 10:12] = q[:, 10:12] - q[:, 1:2] * q[:, 2:4]
    par_ref[0, :, 12:13] = q[:, 12:13] - q[:, 2:3] * q[:, 3:4]
    store.wait()


def local(n_px, n_py, fraction, courant_x, courant_y, courant_z, labels, structure_owner, parcel_owner):
    size_x, size_y, depth = fraction.shape
    structures = structure_owner.shape[1]
    per_owner = structures // n_py
    f32 = jnp.float32
    block = (size_x, size_y, depth)
    moves = 14
    groups = pack_groups(structures)
    packet = (ROWS // groups, groups * structures)
    width = size_y * structures
    any_spec = pl.BlockSpec(memory_space=pl.ANY)
    vmem = pl.BlockSpec(memory_space=pltpu.VMEM)
    dma = pltpu.SemaphoreType.DMA
    limit = 12 * 2**20 + 4 * size_x * width * depth
    rem, total, place = pl.pallas_call(
        functools.partial(kernel, n_px, n_py, structures),
        out_shape=(jax.ShapeDtypeStruct(block, f32), jax.ShapeDtypeStruct(packet, f32),
                   jax.ShapeDtypeStruct((2, structures), f32)),
        in_specs=[pl.BlockSpec(memory_space=pltpu.HBM)] * 7,
        out_specs=(vmem, vmem, vmem),
        scratch_shapes=[
            pltpu.VMEM((size_x + 4, size_y, depth), f32),
            pltpu.VMEM((size_x + 4, size_y, depth), f32),
            pltpu.VMEM((size_x + 1, size_y, depth), f32),
            pltpu.VMEM((size_x + 1, size_y, depth), f32),
            pltpu.VMEM(block, f32),
            pltpu.VMEM(block, f32),
            pltpu.VMEM(block, f32),
            pltpu.VMEM(block, jnp.int32),
            pltpu.VMEM((size_x, width, depth), jnp.bfloat16),
            pltpu.VMEM((FEATURES * 2 * size_y, width), f32),
            pltpu.VMEM((ROWS, width), f32),
            pltpu.VMEM(packet, f32),
            pltpu.VMEM((n_py,) + packet, f32),
            pltpu.VMEM((1, structures), jnp.int32),
            pltpu.VMEM((1, structures), jnp.int32),
            dma((7,)),
            dma((moves,)),
            dma((moves,)),
            dma((n_py,)),
            dma((n_py,)),
        ],
        compiler_params=pltpu.CompilerParams(
            collective_id=0, has_side_effects=True, vmem_limit_bytes=min(limit, 60 * 2**20)),
    )(*[pltpu.with_memory_space_constraint(x, pltpu.HBM)
        for x in (fraction, courant_x, courant_y, courant_z, labels, structure_owner, parcel_owner)])
    small = jax.ShapeDtypeStruct((1, per_owner, 13), f32)
    rem, moments, parcels = pl.pallas_call(
        functools.partial(finish, n_py),
        out_shape=(jax.ShapeDtypeStruct(block, f32), small, small),
        in_specs=[any_spec, vmem, vmem],
        out_specs=(any_spec, vmem, vmem),
        scratch_shapes=[dma(())],
        compiler_params=pltpu.CompilerParams(vmem_limit_bytes=8 * 2**20),
    )(rem, total, place)
    return rem, jnp.swapaxes(moments, 1, 2), jnp.swapaxes(parcels, 1, 2)


def solution(mesh):
    return jax.shard_map(
        functools.partial(local, mesh.shape["px"], mesh.shape["py"]),
        mesh=mesh,
        in_specs=(P("px", "py", None),) * 5 + (P("px", None),) * 2,
        out_specs=(P("px", "py", None), P("px", None, "py"), P("px", None, "py")),
        check_vma=False,
    )
```

```python
import functools

import jax
import jax.numpy as jnp
from jax import lax
from jax.experimental import pallas as pl
from jax.experimental.pallas import tpu as pltpu
from jax.sharding import PartitionSpec as P

MESH = pl.DeviceIdType.MESH
FEATURES = 9
ROWS = 16
EDGE, REST, INNER, OUTER = range(4)


def slope_of(before, centre, after):
    bound = 2.0 * jnp.minimum(centre, 1.0 - centre)
    return jnp.minimum(jnp.maximum(0.5 * (after - before), -bound), bound)


def flux_of(courant, f_low, s_low, f_high, s_high):
    positive = courant > 0.0
    donor = jnp.where(positive, f_low, f_high)
    slope = jnp.where(positive, s_low, -s_high)
    return courant * (donor + 0.5 * (1.0 - jnp.abs(courant)) * slope)


def slot_row(owner, per_owner):
    count = owner.shape[1]
    rows = lax.broadcasted_iota(jnp.int32, (count, count), 0)
    columns = lax.broadcasted_iota(jnp.int32, (count, count), 1)
    wide = jnp.broadcast_to(owner, (count, count)).astype(jnp.float32)
    column = jnp.sum(jnp.where(rows == columns, wide, 0.0), axis=1, keepdims=True)
    earlier = (wide == column) & (rows < columns)
    rank = jnp.sum(jnp.where(earlier, 1.0, 0.0), axis=0, keepdims=True)
    return owner.astype(jnp.float32) * per_owner + rank


def pack_groups(structures):
    return 128 // structures if structures < 128 and 128 % structures == 0 and structures >= 8 else 1


def packed(row_ref, structures):
    width = row_ref.shape[1]
    groups = pack_groups(structures)
    if groups == 1 or width % 128:
        total = row_ref[:, pl.ds(0, structures)]
        for j in range(1, width // structures):
            total = total + row_ref[:, pl.ds(j * structures, structures)]
        if groups == 1:
            return total
        total = jnp.concatenate([total] * groups, axis=1)
    else:
        total = row_ref[:, pl.ds(0, 128)]
        for j in range(1, width // 128):
            total = total + row_ref[:, pl.ds(j * 128, 128)]
        shift = 64
        while shift >= structures:
            total = total + pltpu.roll(total, shift, 1)
            shift //= 2
    rows = ROWS // groups
    lane = lax.broadcasted_iota(jnp.int32, (rows, 128), 1)
    result = total[:rows]
    for k in range(1, groups):
        result = jnp.where(lane >= k * structures, total[k * rows : (k + 1) * rows], result)
    return result


def kernel(
    n_px, n_py,
    structures,
    f_in, cx_in, cy_in, cz_in, lab_in, so_in, po_in,
    rem_ref, total_ref, place_ref,
    p_ref, ex_ref, exc_ref, first_ref, edge_ref, outer_ref, c_ref, cy_ref, cyh_ref, cz_ref, lab_ref, hot_ref, acc_ref,
    row_ref, part_ref, slots_ref, so_ref, po_ref,
    local_sem, halo_send, halo_recv, part_send, part_recv,
):
    size_x, size_y, depth = f_in.shape
    px = lax.axis_index("px")
    py = lax.axis_index("py")
    has_low = py > 0
    has_high = py < n_py - 1

    def device(dx, dy):
        return (lax.rem(px + dx + n_px, n_px), py + dy)

    barrier = pltpu.get_barrier_semaphore()

    def greet(where):
        pl.semaphore_signal(barrier, inc=1, device_id=where, device_id_type=MESH)

    def peer(step):
        return lax.rem(py + step, n_py)

    for dx in (-1, 1):
        greet(device(dx, 0))
    for step in range(1, n_py):
        greet((px, peer(step)))

    loads = [
        (f_in, p_ref.at[pl.ds(2, size_x)]),
        (cx_in, c_ref.at[pl.ds(1, size_x)]),
        (lab_in, lab_ref),
        (cy_in, cy_ref),
        (cz_in, cz_ref),
        (so_in, so_ref),
        (po_in, po_ref),
    ]
    copies = [pltpu.make_async_copy(s, d, local_sem.at[k]) for k, (s, d) in enumerate(loads)]
    for copy in copies:
        copy.start()

    end_x, end_y = size_x - 2, size_y - 2
    last_x, last_y = pl.ds(size_x - 1, 1), pl.ds(size_y - 1, 1)
    low, high = pl.ds(end_y, 2), pl.ds(0, 2)
    top_x, bottom_x, inner_x = pl.ds(end_x, 2), pl.ds(0, 2), pl.ds(2, size_x - 4)
    beyond = pl.ds(size_x + 2, 2)
    moves = []
    for rows in (low, high):
        moves.append((f_in.at[top_x, rows], ex_ref.at[bottom_x, rows], 1, 0, EDGE))
        moves.append((f_in.at[bottom_x, rows], ex_ref.at[pl.ds(2, 2), rows], -1, 0, EDGE))
        moves.append((cx_in.at[last_x, rows], exc_ref.at[:, rows], 1, 0, EDGE))
    moves.append((f_in.at[top_x], p_ref.at[bottom_x], 1, 0, REST))
    moves.append((f_in.at[bottom_x], p_ref.at[beyond], -1, 0, REST))
    moves.append((cx_in.at[last_x], c_ref.at[pl.ds(0, 1)], 1, 0, REST))
    for dy, rows in ((1, low), (-1, high)):
        moves.append((first_ref.at[inner_x, rows], outer_ref.at[inner_x, rows], 0, dy, INNER))
        moves.append((edge_ref.at[pl.ds(0, 2), rows], outer_ref.at[bottom_x, rows], 0, dy, OUTER))
        moves.append((edge_ref.at[pl.ds(2, 2), rows], outer_ref.at[top_x, rows], 0, dy, OUTER))
    moves.append((cy_in.at[:, last_y], cyh_ref.at[:, last_y], 0, 1, INNER))

    remote = [
        pltpu.make_async_remote_copy(
            src_ref=source, dst_ref=target, send_sem=halo_send.at[k], recv_sem=halo_recv.at[k],
            device_id=device(dx, dy), device_id_type=MESH,
        )
        for k, (source, target, dx, dy, group) in enumerate(moves)
    ]

    def for_group(group, action):
        for dy in (0, 1, -1):
            chosen = [c for c, move in zip(remote, moves) if move[3] == dy and move[4] == group]
            if not chosen:
                continue

            def run():
                for copy in chosen:
                    action(copy)

            if dy == 0:
                run()
            else:
                pl.when(has_low if (dy > 0) == (action is wait_arrived) else has_high)(run)

    def start_copy(copy):
        copy.start()

    def wait_sent(copy):
        copy.wait_send()

    def wait_arrived(copy):
        copy.wait_recv()

    def whole_f(k):
        return p_ref[k]

    def whole_c(k):
        return c_ref[k]

    def edge_f(k):
        return ex_ref[k] if k < 2 else p_ref[k] if k < size_x + 2 else ex_ref[k - size_x]

    def edge_c(k):
        return exc_ref[0] if k == 0 else c_ref[k]

    def sweep_x(begin, end, f, c):
        before = slope_of(f(begin), f(begin + 1), f(begin + 2))
        slope = slope_of(f(begin + 1), f(begin + 2), f(begin + 3))
        flux = flux_of(c(begin), f(begin + 1), before, f(begin + 2), slope)
        for i in range(begin, end):
            frac, later, here = f(i + 2), f(i + 3), c(i + 1)
            slope_later = slope_of(frac, later, f(i + 4))
            flux_later = flux_of(here, frac, slope, later, slope_later)
            yield i, frac - (flux_later - flux) + frac * (here - c(i))
            slope, flux = slope_later, flux_later

    for copy in copies[:2]:
        copy.wait()
    for i, value in sweep_x(2, end_x, whole_f, whole_c):
        first_ref[i] = value

    callers = n_py + 1
    pl.semaphore_wait(barrier, callers)
    for_group(EDGE, start_copy)
    for_group(INNER, start_copy)
    for_group(REST, start_copy)

    copies[2].wait()
    names = lax.broadcasted_iota(jnp.int32, (structures, depth), 0)

    def mark(i, carry):
        for j in range(size_y):
            line = jnp.broadcast_to(lab_ref[i, pl.ds(j, 1), :], (structures, depth))
            hot = jnp.where(line == names, 1.0, 0.0).astype(jnp.bfloat16)
            hot_ref[i, pl.ds(j * structures, structures), :] = hot
        return carry

    lax.fori_loop(0, size_x, mark, 0)

    for_group(EDGE, wait_arrived)
    for i, value in sweep_x(0, 2, edge_f, edge_c):
        edge_ref[i] = value
    for i, value in sweep_x(end_x, size_x, edge_f, edge_c):
        edge_ref[i - end_x + 2] = value
    for_group(OUTER, start_copy)

    for copy in copies[3:]:
        copy.wait()
    place_ref[0:1] = slot_row(so_ref[...], structures // n_py)
    place_ref[1:2] = slot_row(po_ref[...], structures // n_py)
    for_group(REST, wait_arrived)
    for begin, end in ((0, 2), (end_x, size_x)):
        for i, value in sweep_x(begin, end, whole_f, whole_c):
            first_ref[i] = value
    for_group(INNER, wait_arrived)

    plane = (size_y, depth)
    sub = lax.broadcasted_iota(jnp.int32, plane, 0)
    lane = lax.broadcasted_iota(jnp.int32, plane, 1)
    first_row, last_row = sub == 0, sub == size_y - 1
    first_cell, last_cell = lane == 0, lane == depth - 1
    low_limit = jnp.where(has_low, end_y, size_y)
    high_limit = jnp.where(has_high, 2, 0)
    halo_valid = (sub >= low_limit) | (sub < high_limit)
    coord_z = (lane.astype(jnp.float32) + 0.5) / depth
    scale = 4.0 / (size_x * size_y * size_y)

    def next_y(main, other):
        return pltpu.roll(jnp.where(first_row, other, main), size_y - 1, 0)

    def prior_y(main, other):
        return pltpu.roll(jnp.where(last_row, other, main), 1, 0)

    def next_z(value):
        return jnp.where(last_cell, 0.0, pltpu.roll(value, depth - 1, 1))

    def prior_z(value):
        return jnp.where(first_cell, 0.0, pltpu.roll(value, 1, 1))

    order = list(range(2, end_x)) + [0, 1, end_x, size_x - 1]
    for step, i in enumerate(order):
        if i == 0:
            for_group(OUTER, wait_arrived)
        first = first_ref[i]
        outer = jnp.where(halo_valid, outer_ref[i], 0.0)
        velocity_x = 0.5 * (c_ref[i + 1] + c_ref[i])

        c = cy_ref[i]
        c_outer = jnp.where(halo_valid, cyh_ref[i], 0.0)
        after, after_outer = next_y(first, outer), next_y(outer, first)
        slope = slope_of(prior_y(first, outer), first, after)
        slope_outer = slope_of(prior_y(outer, first), outer, after_outer)
        flux = flux_of(c, first, slope, after, next_y(slope, slope_outer))
        flux_outer = flux_of(c_outer, outer, slope_outer, after_outer, next_y(slope_outer, slope))
        below = prior_y(c, c_outer)
        second = first - (flux - prior_y(flux, flux_outer)) + first * (c - below)
        velocity_y = 0.5 * (c + below)

        c = cz_ref[i]
        after = next_z(second)
        slope = slope_of(prior_z(second), second, after)
        flux = flux_of(c, second, slope, after, next_z(slope))
        below = prior_z(c)
        third = second - (flux - prior_z(flux)) + second * (c - below)
        velocity_z = 0.5 * (c + below)

        rem_ref[i] = jnp.where(lab_ref[i] >= 0, 0.0, third)
        coord_x = ((px * size_x + i).astype(jnp.float32) + 0.5) / (size_x * n_px)
        w = third * scale
        wx, wz = w * coord_x, w * coord_z
        features = [w, wx, wx * coord_x, wz, wx * coord_z, wz * coord_z,
                    w * velocity_x, w * velocity_y, w * velocity_z]
        parts = []
        for value in features:
            parts.append(value)
            parts.append(value - value.astype(jnp.bfloat16).astype(jnp.float32))
        left = jnp.concatenate(parts, axis=0).astype(jnp.bfloat16)
        sums = lax.dot_general(left, hot_ref[i], (((1,), (1,)), ((), ())),
                               preferred_element_type=jnp.float32)
        if step == 0:
            acc_ref[...] = sums
        else:
            acc_ref[...] += sums

    width = size_y * structures
    sub = lax.broadcasted_iota(jnp.int32, (size_y, width), 0)
    lane = lax.broadcasted_iota(jnp.int32, (size_y, width), 1)
    mine = (lane >= sub * structures) & (lane < (sub + 1) * structures)
    coord_y = ((py * size_y + sub).astype(jnp.float32) + 0.5) / (size_y * n_py)

    def collect(k):
        base = 2 * size_y * k
        both = acc_ref[pl.ds(base, size_y), :] + acc_ref[pl.ds(base + size_y, size_y), :]
        return jnp.where(mine, both, 0.0)

    def put(row, value):
        row_ref[pl.ds(row, 1), :] = jnp.sum(value, axis=0, keepdims=True)

    row_ref[...] = jnp.zeros_like(row_ref)
    w, wx, wxx, wz, wxz, wzz, ux, uy, uz = [collect(k) for k in range(FEATURES)]
    wy = w * coord_y
    for row, value in enumerate((w, wx, wy, wz, ux, uy, uz, wxx, wy * coord_y, wzz,
                                 wx * coord_y, wxz, wz * coord_y)):
        put(row, value)
    total = packed(row_ref, structures)
    part_ref[...] = total
    slots_ref[py] = total

    sends = []
    for step in range(1, n_py):
        copy = pltpu.make_async_remote_copy(
            src_ref=part_ref, dst_ref=slots_ref.at[py],
            send_sem=part_send.at[step], recv_sem=part_recv.at[py],
            device_id=(px, peer(step)), device_id_type=MESH,
        )
        copy.start()
        sends.append(copy)
    for group in (EDGE, INNER, REST, OUTER):
        for_group(group, wait_sent)
    for step in range(1, n_py):
        source = peer(step)
        pltpu.make_async_remote_copy(
            src_ref=part_ref, dst_ref=slots_ref.at[source],
            send_sem=part_send.at[step], recv_sem=part_recv.at[source],
            device_id=(px, source), device_id_type=MESH,
        ).wait_recv()

    total = slots_ref[0]
    for k in range(1, n_py):
        total = total + slots_ref[k]

    total_ref[...] = total
    for copy in sends:
        copy.wait_send()


def finish(n_py, rem_in, total_ref, place_ref, rem_out, mom_ref, par_ref, sem):
    store = pltpu.make_async_copy(rem_in, rem_out, sem)
    store.start()
    structures = place_ref.shape[1]
    per_owner = structures // n_py
    py = lax.axis_index("py")
    groups = pack_groups(structures)
    total = total_ref[...]
    if groups > 1:
        total = jnp.concatenate([total[:, k * structures : (k + 1) * structures] for k in range(groups)], axis=0)

    def pick(slots):
        wanted = lax.broadcasted_iota(jnp.int32, (per_owner, structures), 0) + py * per_owner
        chosen = jnp.where(slots == wanted.astype(jnp.float32), 1.0, 0.0)
        return lax.dot_general(chosen, total, (((1,), (1,)), ((), ())),
                               precision=lax.Precision.HIGHEST, preferred_element_type=jnp.float32)

    mom_ref[0] = pick(place_ref[0:1])[:, :13]
    m = pick(place_ref[1:2])
    volume = m[:, 0:1]
    q = m / jnp.maximum(volume, 0.5)
    centre = q[:, 1:4]
    par_ref[0, :, 0:1] = volume
    par_ref[0, :, 1:7] = q[:, 1:7]
    par_ref[0, :, 7:10] = q[:, 7:10] - centre * centre
    par_ref[0, :, 10:12] = q[:, 10:12] - q[:, 1:2] * q[:, 2:4]
    par_ref[0, :, 12:13] = q[:, 12:13] - q[:, 2:3] * q[:, 3:4]
    store.wait()


def local(n_px, n_py, fraction, courant_x, courant_y, courant_z, labels, structure_owner, parcel_owner):
    size_x, size_y, depth = fraction.shape
    structures = structure_owner.shape[1]
    per_owner = structures // n_py
    f32 = jnp.float32
    block = (size_x, size_y, depth)
    moves = 16
    groups = pack_groups(structures)
    packet = (ROWS // groups, groups * structures)
    width = size_y * structures
    any_spec = pl.BlockSpec(memory_space=pl.ANY)
    vmem = pl.BlockSpec(memory_space=pltpu.VMEM)
    dma = pltpu.SemaphoreType.DMA
    limit = 12 * 2**20 + 4 * size_x * width * depth
    rem, total, place = pl.pallas_call(
        functools.partial(kernel, n_px, n_py, structures),
        out_shape=(jax.ShapeDtypeStruct(block, f32), jax.ShapeDtypeStruct(packet, f32),
                   jax.ShapeDtypeStruct((2, structures), f32)),
        in_specs=[pl.BlockSpec(memory_space=pltpu.HBM)] * 7,
        out_specs=(vmem, vmem, vmem),
        scratch_shapes=[
            pltpu.VMEM((size_x + 4, size_y, depth), f32),
            pltpu.VMEM((4, size_y, depth), f32),
            pltpu.VMEM((1, size_y, depth), f32),
            pltpu.VMEM(block, f32),
            pltpu.VMEM((4, size_y, depth), f32),
            pltpu.VMEM(block, f32),
            pltpu.VMEM((size_x + 1, size_y, depth), f32),
            pltpu.VMEM(block, f32),
            pltpu.VMEM(block, f32),
            pltpu.VMEM(block, f32),
            pltpu.VMEM(block, jnp.int32),
            pltpu.VMEM((size_x, width, depth), jnp.bfloat16),
            pltpu.VMEM((FEATURES * 2 * size_y, width), f32),
            pltpu.VMEM((ROWS, width), f32),
            pltpu.VMEM(packet, f32),
            pltpu.VMEM((n_py,) + packet, f32),
            pltpu.VMEM((1, structures), jnp.int32),
            pltpu.VMEM((1, structures), jnp.int32),
            dma((7,)),
            dma((moves,)),
            dma((moves,)),
            dma((n_py,)),
            dma((n_py,)),
        ],
        compiler_params=pltpu.CompilerParams(
            collective_id=0, has_side_effects=True, vmem_limit_bytes=min(limit, 60 * 2**20)),
    )(*[pltpu.with_memory_space_constraint(x, pltpu.HBM)
        for x in (fraction, courant_x, courant_y, courant_z, labels, structure_owner, parcel_owner)])
    small = jax.ShapeDtypeStruct((1, per_owner, 13), f32)
    rem, moments, parcels = pl.pallas_call(
        functools.partial(finish, n_py),
        out_shape=(jax.ShapeDtypeStruct(block, f32), small, small),
        in_specs=[any_spec, vmem, vmem],
        out_specs=(any_spec, vmem, vmem),
        scratch_shapes=[dma(())],
        compiler_params=pltpu.CompilerParams(vmem_limit_bytes=8 * 2**20),
    )(rem, total, place)
    return rem, jnp.swapaxes(moments, 1, 2), jnp.swapaxes(parcels, 1, 2)


def solution(mesh):
    return jax.shard_map(
        functools.partial(local, mesh.shape["px"], mesh.shape["py"]),
        mesh=mesh,
        in_specs=(P("px", "py", None),) * 5 + (P("px", None),) * 2,
        out_specs=(P("px", "py", None), P("px", None, "py"), P("px", None, "py")),
        check_vma=False,
    )
```

```python
import functools

import jax
import jax.numpy as jnp
from jax import lax
from jax.experimental import pallas as pl
from jax.experimental.pallas import tpu as pltpu
from jax.sharding import PartitionSpec as P

MESH = pl.DeviceIdType.MESH
FEATURES = 9
ROWS = 16
EDGE, REST, INNER, OUTER = range(4)


def slope_of(before, centre, after):
    bound = 2.0 * jnp.minimum(centre, 1.0 - centre)
    return jnp.minimum(jnp.maximum(0.5 * (after - before), -bound), bound)


def flux_of(courant, f_low, s_low, f_high, s_high):
    positive = courant > 0.0
    donor = jnp.where(positive, f_low, f_high)
    slope = jnp.where(positive, s_low, -s_high)
    return courant * (donor + 0.5 * (1.0 - jnp.abs(courant)) * slope)


def slot_row(owner, per_owner):
    count = owner.shape[1]
    rows = lax.broadcasted_iota(jnp.int32, (count, count), 0)
    columns = lax.broadcasted_iota(jnp.int32, (count, count), 1)
    wide = jnp.broadcast_to(owner, (count, count)).astype(jnp.float32)
    column = jnp.sum(jnp.where(rows == columns, wide, 0.0), axis=1, keepdims=True)
    earlier = (wide == column) & (rows < columns)
    rank = jnp.sum(jnp.where(earlier, 1.0, 0.0), axis=0, keepdims=True)
    return owner.astype(jnp.float32) * per_owner + rank


def pack_groups(structures):
    return 128 // structures if structures < 128 and 128 % structures == 0 and structures >= 8 else 1


def packed(row_ref, structures):
    width = row_ref.shape[1]
    groups = pack_groups(structures)
    if groups == 1 or width % 128:
        total = row_ref[:, pl.ds(0, structures)]
        for j in range(1, width // structures):
            total = total + row_ref[:, pl.ds(j * structures, structures)]
        if groups == 1:
            return total
        total = jnp.concatenate([total] * groups, axis=1)
    else:
        total = row_ref[:, pl.ds(0, 128)]
        for j in range(1, width // 128):
            total = total + row_ref[:, pl.ds(j * 128, 128)]
        shift = 64
        while shift >= structures:
            total = total + pltpu.roll(total, shift, 1)
            shift //= 2
    rows = ROWS // groups
    lane = lax.broadcasted_iota(jnp.int32, (rows, 128), 1)
    result = total[:rows]
    for k in range(1, groups):
        result = jnp.where(lane >= k * structures, total[k * rows : (k + 1) * rows], result)
    return result


def kernel(
    n_px, n_py,
    structures,
    f_in, cx_in, cy_in, cz_in, lab_in, so_in, po_in,
    rem_ref, total_ref, place_ref,
    p_ref, ex_ref, exc_ref, first_ref, edge_ref, outer_ref, c_ref, cy_ref, cyh_ref, cz_ref, lab_ref, hot_ref, acc_ref,
    row_ref, part_ref, slots_ref, so_ref, po_ref,
    local_sem, halo_send, halo_recv, part_send, part_recv, go_sem,
):
    size_x, size_y, depth = f_in.shape
    px = lax.axis_index("px")
    py = lax.axis_index("py")
    has_low = py > 0
    has_high = py < n_py - 1

    def device(dx, dy):
        return (lax.rem(px + dx + n_px, n_px), py + dy)

    barrier = pltpu.get_barrier_semaphore()

    def greet(where):
        pl.semaphore_signal(barrier, inc=1, device_id=where, device_id_type=MESH)

    def peer(step):
        return lax.rem(py + step, n_py)

    for dx in (-1, 1):
        greet(device(dx, 0))
    root = n_py // 2
    pl.when(has_low)(lambda: greet((px, py - 1)))
    pl.when(has_high)(lambda: greet((px, py + 1)))
    pl.when((py < root - 1) | (py > root + 1))(lambda: greet((px, root)))

    loads = [
        (f_in, p_ref.at[pl.ds(2, size_x)]),
        (cx_in, c_ref.at[pl.ds(1, size_x)]),
        (lab_in, lab_ref),
        (cy_in, cy_ref),
        (cz_in, cz_ref),
        (so_in, so_ref),
        (po_in, po_ref),
    ]
    copies = [pltpu.make_async_copy(s, d, local_sem.at[k]) for k, (s, d) in enumerate(loads)]
    for copy in copies:
        copy.start()

    end_x, end_y = size_x - 2, size_y - 2
    last_x, last_y = pl.ds(size_x - 1, 1), pl.ds(size_y - 1, 1)
    low, high = pl.ds(end_y, 2), pl.ds(0, 2)
    top_x, bottom_x, inner_x = pl.ds(end_x, 2), pl.ds(0, 2), pl.ds(2, size_x - 4)
    beyond = pl.ds(size_x + 2, 2)
    moves = []
    for rows in (low, high):
        moves.append((p_ref.at[pl.ds(size_x, 2), rows], ex_ref.at[bottom_x, rows], 1, 0, EDGE))
        moves.append((p_ref.at[pl.ds(2, 2), rows], ex_ref.at[pl.ds(2, 2), rows], -1, 0, EDGE))
        moves.append((c_ref.at[pl.ds(size_x, 1), rows], exc_ref.at[:, rows], 1, 0, EDGE))
    moves.append((f_in.at[top_x], p_ref.at[bottom_x], 1, 0, REST))
    moves.append((f_in.at[bottom_x], p_ref.at[beyond], -1, 0, REST))
    moves.append((cx_in.at[last_x], c_ref.at[pl.ds(0, 1)], 1, 0, REST))
    for dy, rows in ((1, low), (-1, high)):
        moves.append((first_ref.at[inner_x, rows], outer_ref.at[inner_x, rows], 0, dy, INNER))
        moves.append((edge_ref.at[pl.ds(0, 2), rows], outer_ref.at[bottom_x, rows], 0, dy, OUTER))
        moves.append((edge_ref.at[pl.ds(2, 2), rows], outer_ref.at[top_x, rows], 0, dy, OUTER))
    moves.append((cy_in.at[:, last_y], cyh_ref.at[:, last_y], 0, 1, INNER))

    remote = [
        pltpu.make_async_remote_copy(
            src_ref=source, dst_ref=target, send_sem=halo_send.at[k], recv_sem=halo_recv.at[k],
            device_id=device(dx, dy), device_id_type=MESH,
        )
        for k, (source, target, dx, dy, group) in enumerate(moves)
    ]

    def for_group(group, action):
        for dy in (0, 1, -1):
            chosen = [c for c, move in zip(remote, moves) if move[3] == dy and move[4] == group]
            if not chosen:
                continue

            def run():
                for copy in chosen:
                    action(copy)

            if dy == 0:
                run()
            else:
                pl.when(has_low if (dy > 0) == (action is wait_arrived) else has_high)(run)

    def start_copy(copy):
        copy.start()

    def wait_sent(copy):
        copy.wait_send()

    def wait_arrived(copy):
        copy.wait_recv()

    def whole_f(k):
        return p_ref[k]

    def whole_c(k):
        return c_ref[k]

    def edge_f(k):
        return ex_ref[k] if k < 2 else p_ref[k] if k < size_x + 2 else ex_ref[k - size_x]

    def edge_c(k):
        return exc_ref[0] if k == 0 else c_ref[k]

    def sweep_x(begin, end, f, c):
        before = slope_of(f(begin), f(begin + 1), f(begin + 2))
        slope = slope_of(f(begin + 1), f(begin + 2), f(begin + 3))
        flux = flux_of(c(begin), f(begin + 1), before, f(begin + 2), slope)
        for i in range(begin, end):
            frac, later, here = f(i + 2), f(i + 3), c(i + 1)
            slope_later = slope_of(frac, later, f(i + 4))
            flux_later = flux_of(here, frac, slope, later, slope_later)
            yield i, frac - (flux_later - flux) + frac * (here - c(i))
            slope, flux = slope_later, flux_later

    for copy in copies[:2]:
        copy.wait()
    for i, value in sweep_x(2, end_x, whole_f, whole_c):
        first_ref[i] = value

    near = 2 + jnp.where(has_low, 1, 0) + jnp.where(has_high, 1, 0)
    pl.semaphore_wait(barrier, jnp.where(py == root, n_py + 1, near))
    for_group(EDGE, start_copy)
    for_group(INNER, start_copy)
    for_group(REST, start_copy)

    @pl.when(py == root)
    def _():
        for step in range(1, n_py):
            pl.semaphore_signal(go_sem, inc=1, device_id=(px, peer(step)), device_id_type=MESH)


    copies[2].wait()
    names = lax.broadcasted_iota(jnp.int32, (structures, depth), 0)

    def mark(i, carry):
        for j in range(size_y):
            line = jnp.broadcast_to(lab_ref[i, pl.ds(j, 1), :], (structures, depth))
            hot = jnp.where(line == names, 1.0, 0.0).astype(jnp.bfloat16)
            hot_ref[i, pl.ds(j * structures, structures), :] = hot
        return carry

    lax.fori_loop(0, size_x, mark, 0)

    for_group(EDGE, wait_arrived)
    for i, value in sweep_x(0, 2, edge_f, edge_c):
        edge_ref[i] = value
    for i, value in sweep_x(end_x, size_x, edge_f, edge_c):
        edge_ref[i - end_x + 2] = value
    for_group(OUTER, start_copy)

    for copy in copies[3:]:
        copy.wait()
    place_ref[0:1] = slot_row(so_ref[...], structures // n_py)
    place_ref[1:2] = slot_row(po_ref[...], structures // n_py)
    for_group(REST, wait_arrived)
    for begin, end in ((0, 2), (end_x, size_x)):
        for i, value in sweep_x(begin, end, whole_f, whole_c):
            first_ref[i] = value
    for_group(INNER, wait_arrived)

    plane = (size_y, depth)
    sub = lax.broadcasted_iota(jnp.int32, plane, 0)
    lane = lax.broadcasted_iota(jnp.int32, plane, 1)
    first_row, last_row = sub == 0, sub == size_y - 1
    first_cell, last_cell = lane == 0, lane == depth - 1
    low_limit = jnp.where(has_low, end_y, size_y)
    high_limit = jnp.where(has_high, 2, 0)
    halo_valid = (sub >= low_limit) | (sub < high_limit)
    coord_z = (lane.astype(jnp.float32) + 0.5) / depth
    scale = 4.0 / (size_x * size_y * size_y)

    def next_y(main, other):
        return pltpu.roll(jnp.where(first_row, other, main), size_y - 1, 0)

    def prior_y(main, other):
        return pltpu.roll(jnp.where(last_row, other, main), 1, 0)

    def next_z(value):
        return jnp.where(last_cell, 0.0, pltpu.roll(value, depth - 1, 1))

    def prior_z(value):
        return jnp.where(first_cell, 0.0, pltpu.roll(value, 1, 1))

    order = list(range(2, end_x)) + [0, 1, end_x, size_x - 1]
    for step, i in enumerate(order):
        if i == 0:
            for_group(OUTER, wait_arrived)
        first = first_ref[i]
        outer = jnp.where(halo_valid, outer_ref[i], 0.0)
        velocity_x = 0.5 * (c_ref[i + 1] + c_ref[i])

        c = cy_ref[i]
        c_outer = jnp.where(halo_valid, cyh_ref[i], 0.0)
        after, after_outer = next_y(first, outer), next_y(outer, first)
        slope = slope_of(prior_y(first, outer), first, after)
        slope_outer = slope_of(prior_y(outer, first), outer, after_outer)
        flux = flux_of(c, first, slope, after, next_y(slope, slope_outer))
        flux_outer = flux_of(c_outer, outer, slope_outer, after_outer, next_y(slope_outer, slope))
        below = prior_y(c, c_outer)
        second = first - (flux - prior_y(flux, flux_outer)) + first * (c - below)
        velocity_y = 0.5 * (c + below)

        c = cz_ref[i]
        after = next_z(second)
        slope = slope_of(prior_z(second), second, after)
        flux = flux_of(c, second, slope, after, next_z(slope))
        below = prior_z(c)
        third = second - (flux - prior_z(flux)) + second * (c - below)
        velocity_z = 0.5 * (c + below)

        rem_ref[i] = jnp.where(lab_ref[i] >= 0, 0.0, third)
        coord_x = ((px * size_x + i).astype(jnp.float32) + 0.5) / (size_x * n_px)
        w = third * scale
        wx, wz = w * coord_x, w * coord_z
        features = [w, wx, wx * coord_x, wz, wx * coord_z, wz * coord_z,
                    w * velocity_x, w * velocity_y, w * velocity_z]
        parts = []
        for value in features:
            parts.append(value)
            parts.append(value - value.astype(jnp.bfloat16).astype(jnp.float32))
        left = jnp.concatenate(parts, axis=0).astype(jnp.bfloat16)
        sums = lax.dot_general(left, hot_ref[i], (((1,), (1,)), ((), ())),
                               preferred_element_type=jnp.float32)
        if step == 0:
            acc_ref[...] = sums
        else:
            acc_ref[...] += sums

    width = size_y * structures
    sub = lax.broadcasted_iota(jnp.int32, (size_y, width), 0)
    lane = lax.broadcasted_iota(jnp.int32, (size_y, width), 1)
    mine = (lane >= sub * structures) & (lane < (sub + 1) * structures)
    coord_y = ((py * size_y + sub).astype(jnp.float32) + 0.5) / (size_y * n_py)

    def collect(k):
        base = 2 * size_y * k
        both = acc_ref[pl.ds(base, size_y), :] + acc_ref[pl.ds(base + size_y, size_y), :]
        return jnp.where(mine, both, 0.0)

    def put(row, value):
        row_ref[pl.ds(row, 1), :] = jnp.sum(value, axis=0, keepdims=True)

    row_ref[...] = jnp.zeros_like(row_ref)
    w, wx, wxx, wz, wxz, wzz, ux, uy, uz = [collect(k) for k in range(FEATURES)]
    wy = w * coord_y
    for row, value in enumerate((w, wx, wy, wz, ux, uy, uz, wxx, wy * coord_y, wzz,
                                 wx * coord_y, wxz, wz * coord_y)):
        put(row, value)
    total = packed(row_ref, structures)
    part_ref[...] = total
    slots_ref[py] = total

    pl.when(py != root)(lambda: pl.semaphore_wait(go_sem, 1))
    sends = []
    for step in range(1, n_py):
        copy = pltpu.make_async_remote_copy(
            src_ref=part_ref, dst_ref=slots_ref.at[py],
            send_sem=part_send.at[step], recv_sem=part_recv.at[py],
            device_id=(px, peer(step)), device_id_type=MESH,
        )
        copy.start()
        sends.append(copy)
    for group in (EDGE, INNER, REST, OUTER):
        for_group(group, wait_sent)
    for step in range(1, n_py):
        source = peer(step)
        pltpu.make_async_remote_copy(
            src_ref=part_ref, dst_ref=slots_ref.at[source],
            send_sem=part_send.at[step], recv_sem=part_recv.at[source],
            device_id=(px, source), device_id_type=MESH,
        ).wait_recv()

    total = slots_ref[0]
    for k in range(1, n_py):
        total = total + slots_ref[k]

    total_ref[...] = total
    for copy in sends:
        copy.wait_send()


def finish(n_py, rem_in, total_ref, place_ref, rem_out, mom_ref, par_ref, sem):
    store = pltpu.make_async_copy(rem_in, rem_out, sem)
    store.start()
    structures = place_ref.shape[1]
    per_owner = structures // n_py
    py = lax.axis_index("py")
    groups = pack_groups(structures)
    total = total_ref[...]
    if groups > 1:
        total = jnp.concatenate([total[:, k * structures : (k + 1) * structures] for k in range(groups)], axis=0)

    def pick(slots):
        wanted = lax.broadcasted_iota(jnp.int32, (per_owner, structures), 0) + py * per_owner
        chosen = jnp.where(slots == wanted.astype(jnp.float32), 1.0, 0.0)
        return lax.dot_general(chosen, total, (((1,), (1,)), ((), ())),
                               precision=lax.Precision.HIGHEST, preferred_element_type=jnp.float32)

    mom_ref[0] = pick(place_ref[0:1])[:, :13]
    m = pick(place_ref[1:2])
    volume = m[:, 0:1]
    q = m / jnp.maximum(volume, 0.5)
    centre = q[:, 1:4]
    par_ref[0, :, 0:1] = volume
    par_ref[0, :, 1:7] = q[:, 1:7]
    par_ref[0, :, 7:10] = q[:, 7:10] - centre * centre
    par_ref[0, :, 10:12] = q[:, 10:12] - q[:, 1:2] * q[:, 2:4]
    par_ref[0, :, 12:13] = q[:, 12:13] - q[:, 2:3] * q[:, 3:4]
    store.wait()


def local(n_px, n_py, fraction, courant_x, courant_y, courant_z, labels, structure_owner, parcel_owner):
    size_x, size_y, depth = fraction.shape
    structures = structure_owner.shape[1]
    per_owner = structures // n_py
    f32 = jnp.float32
    block = (size_x, size_y, depth)
    moves = 16
    groups = pack_groups(structures)
    packet = (ROWS // groups, groups * structures)
    width = size_y * structures
    any_spec = pl.BlockSpec(memory_space=pl.ANY)
    vmem = pl.BlockSpec(memory_space=pltpu.VMEM)
    dma = pltpu.SemaphoreType.DMA
    limit = 12 * 2**20 + 4 * size_x * width * depth
    rem, total, place = pl.pallas_call(
        functools.partial(kernel, n_px, n_py, structures),
        out_shape=(jax.ShapeDtypeStruct(block, f32), jax.ShapeDtypeStruct(packet, f32),
                   jax.ShapeDtypeStruct((2, structures), f32)),
        in_specs=[pl.BlockSpec(memory_space=pltpu.HBM)] * 7,
        out_specs=(vmem, vmem, vmem),
        scratch_shapes=[
            pltpu.VMEM((size_x + 4, size_y, depth), f32),
            pltpu.VMEM((4, size_y, depth), f32),
            pltpu.VMEM((1, size_y, depth), f32),
            pltpu.VMEM(block, f32),
            pltpu.VMEM((4, size_y, depth), f32),
            pltpu.VMEM(block, f32),
            pltpu.VMEM((size_x + 1, size_y, depth), f32),
            pltpu.VMEM(block, f32),
            pltpu.VMEM(block, f32),
            pltpu.VMEM(block, f32),
            pltpu.VMEM(block, jnp.int32),
            pltpu.VMEM((size_x, width, depth), jnp.bfloat16),
            pltpu.VMEM((FEATURES * 2 * size_y, width), f32),
            pltpu.VMEM((ROWS, width), f32),
            pltpu.VMEM(packet, f32),
            pltpu.VMEM((n_py,) + packet, f32),
            pltpu.VMEM((1, structures), jnp.int32),
            pltpu.VMEM((1, structures), jnp.int32),
            dma((7,)),
            dma((moves,)),
            dma((moves,)),
            dma((n_py,)),
            dma((n_py,)),
            pltpu.SemaphoreType.REGULAR,
        ],
        compiler_params=pltpu.CompilerParams(
            collective_id=0, has_side_effects=True, vmem_limit_bytes=min(limit, 60 * 2**20)),
    )(*[pltpu.with_memory_space_constraint(x, pltpu.HBM)
        for x in (fraction, courant_x, courant_y, courant_z, labels, structure_owner, parcel_owner)])
    small = jax.ShapeDtypeStruct((1, per_owner, 13), f32)
    rem, moments, parcels = pl.pallas_call(
        functools.partial(finish, n_py),
        out_shape=(jax.ShapeDtypeStruct(block, f32), small, small),
        in_specs=[any_spec, vmem, vmem],
        out_specs=(any_spec, vmem, vmem),
        scratch_shapes=[dma(())],
        compiler_params=pltpu.CompilerParams(vmem_limit_bytes=8 * 2**20),
    )(rem, total, place)
    return rem, jnp.swapaxes(moments, 1, 2), jnp.swapaxes(parcels, 1, 2)


def solution(mesh):
    return jax.shard_map(
        functools.partial(local, mesh.shape["px"], mesh.shape["py"]),
        mesh=mesh,
        in_specs=(P("px", "py", None),) * 5 + (P("px", None),) * 2,
        out_specs=(P("px", "py", None), P("px", None, "py"), P("px", None, "py")),
        check_vma=False,
    )
```

```python
import functools

import jax
import jax.numpy as jnp
from jax import lax
from jax.experimental import pallas as pl
from jax.experimental.pallas import tpu as pltpu
from jax.sharding import PartitionSpec as P

MESH = pl.DeviceIdType.MESH
FEATURES = 9
ROWS = 16
EDGE_LOW, EDGE_HIGH, REST, INNER, OUTER_LOW, OUTER_HIGH = range(6)


def slope_of(before, centre, after):
    bound = 2.0 * jnp.minimum(centre, 1.0 - centre)
    return jnp.minimum(jnp.maximum(0.5 * (after - before), -bound), bound)


def flux_of(courant, f_low, s_low, f_high, s_high):
    positive = courant > 0.0
    donor = jnp.where(positive, f_low, f_high)
    slope = jnp.where(positive, s_low, -s_high)
    return courant * (donor + 0.5 * (1.0 - jnp.abs(courant)) * slope)


def slot_row(owner, per_owner):
    count = owner.shape[1]
    rows = lax.broadcasted_iota(jnp.int32, (count, count), 0)
    columns = lax.broadcasted_iota(jnp.int32, (count, count), 1)
    wide = jnp.broadcast_to(owner, (count, count)).astype(jnp.float32)
    column = jnp.sum(jnp.where(rows == columns, wide, 0.0), axis=1, keepdims=True)
    earlier = (wide == column) & (rows < columns)
    rank = jnp.sum(jnp.where(earlier, 1.0, 0.0), axis=0, keepdims=True)
    return owner.astype(jnp.float32) * per_owner + rank


def pack_groups(structures):
    return 128 // structures if structures < 128 and 128 % structures == 0 and structures >= 8 else 1


def packed(row_ref, structures):
    width = row_ref.shape[1]
    groups = pack_groups(structures)
    if groups == 1 or width % 128:
        total = row_ref[:, pl.ds(0, structures)]
        for j in range(1, width // structures):
            total = total + row_ref[:, pl.ds(j * structures, structures)]
        if groups == 1:
            return total
        total = jnp.concatenate([total] * groups, axis=1)
    else:
        total = row_ref[:, pl.ds(0, 128)]
        for j in range(1, width // 128):
            total = total + row_ref[:, pl.ds(j * 128, 128)]
        shift = 64
        while shift >= structures:
            total = total + pltpu.roll(total, shift, 1)
            shift //= 2
    rows = ROWS // groups
    lane = lax.broadcasted_iota(jnp.int32, (rows, 128), 1)
    result = total[:rows]
    for k in range(1, groups):
        result = jnp.where(lane >= k * structures, total[k * rows : (k + 1) * rows], result)
    return result


def kernel(
    n_px, n_py,
    structures,
    f_in, cx_in, cy_in, cz_in, lab_in, so_in, po_in,
    rem_ref, total_ref, place_ref,
    p_ref, ex_ref, exc_ref, first_ref, edge_ref, outer_ref, c_ref, cy_ref, cyh_ref, cz_ref, lab_ref, hot_ref, acc_ref,
    row_ref, part_ref, slots_ref, so_ref, po_ref,
    local_sem, halo_send, halo_recv, part_send, part_recv, go_sem,
):
    size_x, size_y, depth = f_in.shape
    px = lax.axis_index("px")
    py = lax.axis_index("py")
    has_low = py > 0
    has_high = py < n_py - 1

    def device(dx, dy):
        return (lax.rem(px + dx + n_px, n_px), py + dy)

    barrier = pltpu.get_barrier_semaphore()

    def greet(where):
        pl.semaphore_signal(barrier, inc=1, device_id=where, device_id_type=MESH)

    def peer(step):
        return lax.rem(py + step, n_py)

    for dx in (-1, 1):
        greet(device(dx, 0))
    root = n_py // 2
    pl.when(has_low)(lambda: greet((px, py - 1)))
    pl.when(has_high)(lambda: greet((px, py + 1)))
    pl.when((py < root - 1) | (py > root + 1))(lambda: greet((px, root)))

    loads = [
        (f_in, p_ref.at[pl.ds(2, size_x)]),
        (cx_in, c_ref.at[pl.ds(1, size_x)]),
        (lab_in, lab_ref),
        (cy_in, cy_ref),
        (cz_in, cz_ref),
        (so_in, so_ref),
        (po_in, po_ref),
    ]
    copies = [pltpu.make_async_copy(s, d, local_sem.at[k]) for k, (s, d) in enumerate(loads)]
    for copy in copies:
        copy.start()

    end_x, end_y = size_x - 2, size_y - 2
    last_x, last_y = pl.ds(size_x - 1, 1), pl.ds(size_y - 1, 1)
    low, high = pl.ds(end_y, 2), pl.ds(0, 2)
    top_x, bottom_x, inner_x = pl.ds(end_x, 2), pl.ds(0, 2), pl.ds(2, size_x - 4)
    beyond = pl.ds(size_x + 2, 2)
    moves = []
    for rows in (low, high):
        moves.append((p_ref.at[pl.ds(size_x, 2), rows], ex_ref.at[bottom_x, rows], 1, 0, EDGE_LOW))
        moves.append((p_ref.at[pl.ds(2, 2), rows], ex_ref.at[pl.ds(2, 2), rows], -1, 0, EDGE_HIGH))
        moves.append((c_ref.at[pl.ds(size_x, 1), rows], exc_ref.at[:, rows], 1, 0, EDGE_LOW))
    moves.append((f_in.at[top_x], p_ref.at[bottom_x], 1, 0, REST))
    moves.append((f_in.at[bottom_x], p_ref.at[beyond], -1, 0, REST))
    moves.append((cx_in.at[last_x], c_ref.at[pl.ds(0, 1)], 1, 0, REST))
    for dy, rows in ((1, low), (-1, high)):
        moves.append((first_ref.at[inner_x, rows], outer_ref.at[inner_x, rows], 0, dy, INNER))
        moves.append((edge_ref.at[pl.ds(0, 2), rows], outer_ref.at[bottom_x, rows], 0, dy, OUTER_LOW))
        moves.append((edge_ref.at[pl.ds(2, 2), rows], outer_ref.at[top_x, rows], 0, dy, OUTER_HIGH))
    moves.append((cy_in.at[:, last_y], cyh_ref.at[:, last_y], 0, 1, INNER))

    remote = [
        pltpu.make_async_remote_copy(
            src_ref=source, dst_ref=target, send_sem=halo_send.at[k], recv_sem=halo_recv.at[k],
            device_id=device(dx, dy), device_id_type=MESH,
        )
        for k, (source, target, dx, dy, group) in enumerate(moves)
    ]

    def for_group(group, action):
        for dy in (0, 1, -1):
            chosen = [c for c, move in zip(remote, moves) if move[3] == dy and move[4] == group]
            if not chosen:
                continue

            def run():
                for copy in chosen:
                    action(copy)

            if dy == 0:
                run()
            else:
                pl.when(has_low if (dy > 0) == (action is wait_arrived) else has_high)(run)

    def start_copy(copy):
        copy.start()

    def wait_sent(copy):
        copy.wait_send()

    def wait_arrived(copy):
        copy.wait_recv()

    def whole_f(k):
        return p_ref[k]

    def whole_c(k):
        return c_ref[k]

    def edge_f(k):
        return ex_ref[k] if k < 2 else p_ref[k] if k < size_x + 2 else ex_ref[k - size_x]

    def edge_c(k):
        return exc_ref[0] if k == 0 else c_ref[k]

    def sweep_x(begin, end, f, c):
        before = slope_of(f(begin), f(begin + 1), f(begin + 2))
        slope = slope_of(f(begin + 1), f(begin + 2), f(begin + 3))
        flux = flux_of(c(begin), f(begin + 1), before, f(begin + 2), slope)
        for i in range(begin, end):
            frac, later, here = f(i + 2), f(i + 3), c(i + 1)
            slope_later = slope_of(frac, later, f(i + 4))
            flux_later = flux_of(here, frac, slope, later, slope_later)
            yield i, frac - (flux_later - flux) + frac * (here - c(i))
            slope, flux = slope_later, flux_later

    for copy in copies[:2]:
        copy.wait()
    for i, value in sweep_x(2, end_x, whole_f, whole_c):
        first_ref[i] = value

    near = 2 + jnp.where(has_low, 1, 0) + jnp.where(has_high, 1, 0)
    pl.semaphore_wait(barrier, jnp.where(py == root, n_py + 1, near))
    for_group(EDGE_LOW, start_copy)
    for_group(EDGE_HIGH, start_copy)
    for_group(INNER, start_copy)
    for_group(REST, start_copy)

    @pl.when(py == root)
    def _():
        for step in range(1, n_py):
            pl.semaphore_signal(go_sem, inc=1, device_id=(px, peer(step)), device_id_type=MESH)


    copies[2].wait()
    names = lax.broadcasted_iota(jnp.int32, (structures, depth), 0)

    def mark(i, carry):
        for j in range(size_y):
            line = jnp.broadcast_to(lab_ref[i, pl.ds(j, 1), :], (structures, depth))
            hot = jnp.where(line == names, 1.0, 0.0).astype(jnp.bfloat16)
            hot_ref[i, pl.ds(j * structures, structures), :] = hot
        return carry

    lax.fori_loop(0, size_x, mark, 0)

    even = lax.rem(px, 2) == 0

    def lower():
        for_group(EDGE_LOW, wait_arrived)
        for i, value in sweep_x(0, 2, edge_f, edge_c):
            edge_ref[i] = value
        for_group(OUTER_LOW, start_copy)

    def upper():
        for_group(EDGE_HIGH, wait_arrived)
        for i, value in sweep_x(end_x, size_x, edge_f, edge_c):
            edge_ref[i - end_x + 2] = value
        for_group(OUTER_HIGH, start_copy)

    @pl.when(even)
    def _():
        upper()
        lower()

    @pl.when(jnp.logical_not(even))
    def _():
        lower()
        upper()

    for copy in copies[3:]:
        copy.wait()
    place_ref[0:1] = slot_row(so_ref[...], structures // n_py)
    place_ref[1:2] = slot_row(po_ref[...], structures // n_py)
    for_group(REST, wait_arrived)
    for begin, end in ((0, 2), (end_x, size_x)):
        for i, value in sweep_x(begin, end, whole_f, whole_c):
            first_ref[i] = value
    for_group(INNER, wait_arrived)

    plane = (size_y, depth)
    sub = lax.broadcasted_iota(jnp.int32, plane, 0)
    lane = lax.broadcasted_iota(jnp.int32, plane, 1)
    first_row, last_row = sub == 0, sub == size_y - 1
    first_cell, last_cell = lane == 0, lane == depth - 1
    low_limit = jnp.where(has_low, end_y, size_y)
    high_limit = jnp.where(has_high, 2, 0)
    halo_valid = (sub >= low_limit) | (sub < high_limit)
    coord_z = (lane.astype(jnp.float32) + 0.5) / depth
    scale = 4.0 / (size_x * size_y * size_y)

    def next_y(main, other):
        return pltpu.roll(jnp.where(first_row, other, main), size_y - 1, 0)

    def prior_y(main, other):
        return pltpu.roll(jnp.where(last_row, other, main), 1, 0)

    def next_z(value):
        return jnp.where(last_cell, 0.0, pltpu.roll(value, depth - 1, 1))

    def prior_z(value):
        return jnp.where(first_cell, 0.0, pltpu.roll(value, 1, 1))

    bottom, top = [0, 1], [end_x, end_x + 1]

    def await_side(group, chosen):
        pl.when(chosen)(lambda: for_group(group, wait_arrived))

    for step in range(size_x):
        k = step - (size_x - 4)
        if k < 0:
            i = step + 2
        else:
            if k == 0 or k == 2:
                await_side(OUTER_HIGH, even if k == 0 else jnp.logical_not(even))
                await_side(OUTER_LOW, even if k == 2 else jnp.logical_not(even))
            i = jnp.where(even, (top + bottom)[k], (bottom + top)[k])
        first = first_ref[i]
        outer = jnp.where(halo_valid, outer_ref[i], 0.0)
        velocity_x = 0.5 * (c_ref[i + 1] + c_ref[i])

        c = cy_ref[i]
        c_outer = jnp.where(halo_valid, cyh_ref[i], 0.0)
        after, after_outer = next_y(first, outer), next_y(outer, first)
        slope = slope_of(prior_y(first, outer), first, after)
        slope_outer = slope_of(prior_y(outer, first), outer, after_outer)
        flux = flux_of(c, first, slope, after, next_y(slope, slope_outer))
        flux_outer = flux_of(c_outer, outer, slope_outer, after_outer, next_y(slope_outer, slope))
        below = prior_y(c, c_outer)
        second = first - (flux - prior_y(flux, flux_outer)) + first * (c - below)
        velocity_y = 0.5 * (c + below)

        c = cz_ref[i]
        after = next_z(second)
        slope = slope_of(prior_z(second), second, after)
        flux = flux_of(c, second, slope, after, next_z(slope))
        below = prior_z(c)
        third = second - (flux - prior_z(flux)) + second * (c - below)
        velocity_z = 0.5 * (c + below)

        rem_ref[i] = jnp.where(lab_ref[i] >= 0, 0.0, third)
        coord_x = ((px * size_x + i).astype(jnp.float32) + 0.5) / (size_x * n_px)
        w = third * scale
        wx, wz = w * coord_x, w * coord_z
        features = [w, wx, wx * coord_x, wz, wx * coord_z, wz * coord_z,
                    w * velocity_x, w * velocity_y, w * velocity_z]
        parts = []
        for value in features:
            parts.append(value)
            parts.append(value - value.astype(jnp.bfloat16).astype(jnp.float32))
        left = jnp.concatenate(parts, axis=0).astype(jnp.bfloat16)
        sums = lax.dot_general(left, hot_ref[i], (((1,), (1,)), ((), ())),
                               preferred_element_type=jnp.float32)
        if step == 0:
            acc_ref[...] = sums
        else:
            acc_ref[...] += sums

    width = size_y * structures
    sub = lax.broadcasted_iota(jnp.int32, (size_y, width), 0)
    lane = lax.broadcasted_iota(jnp.int32, (size_y, width), 1)
    mine = (lane >= sub * structures) & (lane < (sub + 1) * structures)
    coord_y = ((py * size_y + sub).astype(jnp.float32) + 0.5) / (size_y * n_py)

    def collect(k):
        base = 2 * size_y * k
        both = acc_ref[pl.ds(base, size_y), :] + acc_ref[pl.ds(base + size_y, size_y), :]
        return jnp.where(mine, both, 0.0)

    def put(row, value):
        row_ref[pl.ds(row, 1), :] = jnp.sum(value, axis=0, keepdims=True)

    row_ref[...] = jnp.zeros_like(row_ref)
    w, wx, wxx, wz, wxz, wzz, ux, uy, uz = [collect(k) for k in range(FEATURES)]
    wy = w * coord_y
    for row, value in enumerate((w, wx, wy, wz, ux, uy, uz, wxx, wy * coord_y, wzz,
                                 wx * coord_y, wxz, wz * coord_y)):
        put(row, value)
    total = packed(row_ref, structures)
    part_ref[...] = total
    slots_ref[py] = total

    pl.when(py != root)(lambda: pl.semaphore_wait(go_sem, 1))
    sends = []
    for step in range(1, n_py):
        copy = pltpu.make_async_remote_copy(
            src_ref=part_ref, dst_ref=slots_ref.at[py],
            send_sem=part_send.at[step], recv_sem=part_recv.at[py],
            device_id=(px, peer(step)), device_id_type=MESH,
        )
        copy.start()
        sends.append(copy)
    for group in (EDGE_LOW, EDGE_HIGH, INNER, REST, OUTER_LOW, OUTER_HIGH):
        for_group(group, wait_sent)
    for step in range(1, n_py):
        source = peer(step)
        pltpu.make_async_remote_copy(
            src_ref=part_ref, dst_ref=slots_ref.at[source],
            send_sem=part_send.at[step], recv_sem=part_recv.at[source],
            device_id=(px, source), device_id_type=MESH,
        ).wait_recv()

    total = slots_ref[0]
    for k in range(1, n_py):
        total = total + slots_ref[k]

    total_ref[...] = total
    for copy in sends:
        copy.wait_send()


def finish(n_py, rem_in, total_ref, place_ref, rem_out, mom_ref, par_ref, sem):
    store = pltpu.make_async_copy(rem_in, rem_out, sem)
    store.start()
    structures = place_ref.shape[1]
    per_owner = structures // n_py
    py = lax.axis_index("py")
    groups = pack_groups(structures)
    total = total_ref[...]
    if groups > 1:
        total = jnp.concatenate([total[:, k * structures : (k + 1) * structures] for k in range(groups)], axis=0)

    def pick(slots):
        wanted = lax.broadcasted_iota(jnp.int32, (per_owner, structures), 0) + py * per_owner
        chosen = jnp.where(slots == wanted.astype(jnp.float32), 1.0, 0.0)
        return lax.dot_general(chosen, total, (((1,), (1,)), ((), ())),
                               precision=lax.Precision.HIGHEST, preferred_element_type=jnp.float32)

    mom_ref[0] = pick(place_ref[0:1])[:, :13]
    m = pick(place_ref[1:2])
    volume = m[:, 0:1]
    q = m / jnp.maximum(volume, 0.5)
    centre = q[:, 1:4]
    par_ref[0, :, 0:1] = volume
    par_ref[0, :, 1:7] = q[:, 1:7]
    par_ref[0, :, 7:10] = q[:, 7:10] - centre * centre
    par_ref[0, :, 10:12] = q[:, 10:12] - q[:, 1:2] * q[:, 2:4]
    par_ref[0, :, 12:13] = q[:, 12:13] - q[:, 2:3] * q[:, 3:4]
    store.wait()


def local(n_px, n_py, fraction, courant_x, courant_y, courant_z, labels, structure_owner, parcel_owner):
    size_x, size_y, depth = fraction.shape
    structures = structure_owner.shape[1]
    per_owner = structures // n_py
    f32 = jnp.float32
    block = (size_x, size_y, depth)
    moves = 16
    groups = pack_groups(structures)
    packet = (ROWS // groups, groups * structures)
    width = size_y * structures
    any_spec = pl.BlockSpec(memory_space=pl.ANY)
    vmem = pl.BlockSpec(memory_space=pltpu.VMEM)
    dma = pltpu.SemaphoreType.DMA
    limit = 12 * 2**20 + 4 * size_x * width * depth
    rem, total, place = pl.pallas_call(
        functools.partial(kernel, n_px, n_py, structures),
        out_shape=(jax.ShapeDtypeStruct(block, f32), jax.ShapeDtypeStruct(packet, f32),
                   jax.ShapeDtypeStruct((2, structures), f32)),
        in_specs=[pl.BlockSpec(memory_space=pltpu.HBM)] * 7,
        out_specs=(vmem, vmem, vmem),
        scratch_shapes=[
            pltpu.VMEM((size_x + 4, size_y, depth), f32),
            pltpu.VMEM((4, size_y, depth), f32),
            pltpu.VMEM((1, size_y, depth), f32),
            pltpu.VMEM(block, f32),
            pltpu.VMEM((4, size_y, depth), f32),
            pltpu.VMEM(block, f32),
            pltpu.VMEM((size_x + 1, size_y, depth), f32),
            pltpu.VMEM(block, f32),
            pltpu.VMEM(block, f32),
            pltpu.VMEM(block, f32),
            pltpu.VMEM(block, jnp.int32),
            pltpu.VMEM((size_x, width, depth), jnp.bfloat16),
            pltpu.VMEM((FEATURES * 2 * size_y, width), f32),
            pltpu.VMEM((ROWS, width), f32),
            pltpu.VMEM(packet, f32),
            pltpu.VMEM((n_py,) + packet, f32),
            pltpu.VMEM((1, structures), jnp.int32),
            pltpu.VMEM((1, structures), jnp.int32),
            dma((7,)),
            dma((moves,)),
            dma((moves,)),
            dma((n_py,)),
            dma((n_py,)),
            pltpu.SemaphoreType.REGULAR,
        ],
        compiler_params=pltpu.CompilerParams(
            collective_id=0, has_side_effects=True, vmem_limit_bytes=min(limit, 60 * 2**20)),
    )(*[pltpu.with_memory_space_constraint(x, pltpu.HBM)
        for x in (fraction, courant_x, courant_y, courant_z, labels, structure_owner, parcel_owner)])
    small = jax.ShapeDtypeStruct((1, per_owner, 13), f32)
    rem, moments, parcels = pl.pallas_call(
        functools.partial(finish, n_py),
        out_shape=(jax.ShapeDtypeStruct(block, f32), small, small),
        in_specs=[any_spec, vmem, vmem],
        out_specs=(any_spec, vmem, vmem),
        scratch_shapes=[dma(())],
        compiler_params=pltpu.CompilerParams(vmem_limit_bytes=8 * 2**20),
    )(rem, total, place)
    return rem, jnp.swapaxes(moments, 1, 2), jnp.swapaxes(parcels, 1, 2)


def solution(mesh):
    return jax.shard_map(
        functools.partial(local, mesh.shape["px"], mesh.shape["py"]),
        mesh=mesh,
        in_specs=(P("px", "py", None),) * 5 + (P("px", None),) * 2,
        out_specs=(P("px", "py", None), P("px", None, "py"), P("px", None, "py")),
        check_vma=False,
    )
```
